32 devices in a mesh: seq: 8 (over z, y), tp: 4 (over x, core).
Axes of the slice: x: 2, y: 2, z: 4, core: 2. Of those that a mesh axis runs over, the one named last changes fastest.
Arguments:
- hidden: bfloat16 [1024, 4096], P('seq', 'tp'), may hold values from -6 to 6
- w_proj: bfloat16 [4096, 1024], P('tp'), may hold values from -1 to 1
- codes: int32 [1024, 4], P('seq'), may hold values from 0 to 2047
- embed_table: bfloat16 [3, 2048, 1024], P(None, None, 'tp'), may hold values from -6 to 6
- w_qkv: bfloat16 [1024, 3, 1024], P(None, None, 'tp'), may hold values from -1 to 1
- w_out: bfloat16 [1024, 1024], P('tp'), may hold values from -0.1875 to 0.1875
- head_table: bfloat16 [4, 1024, 2048], P(None, None, 'tp'), may hold values from -1 to 1
- gain_attn: float32 [1024], replicated, may hold values from 0.5 to 1.5
- gain_head: float32 [1024], replicated, may hold values from 0.5 to 1.5
Outputs:
- row_loss: float32 [1024, 4], P('seq')
- grad_hidden: bfloat16 [1024, 4096], P('seq', 'tp')
- grad_proj: float32 [4096, 1024], P('tp', 'seq')
The draws below stay inside these ranges and needn't reach their ends.
All inputs are finite; a program needn't handle non-finite values.
Results may differ from the reference program's by a relative error of at most 0.02.
Values may be sent and summed in bfloat16 or wider, within the bound.
No kernel may reach another device: no remote copies, remote signals or barrier semaphores. Data moves between devices by JAX's collectives and lax.ppermute only.
A program may use at most 64 MiB of HBM per device.

```python
import jax
import jax.numpy as jnp
from jax import lax

DT = 4096
DD = 1024
V = 2048
HEADS = 16
KW = 4
FRAMES = 1024


def draw_hidden(key, part):
    drawn = jax.random.truncated_normal(jax.random.fold_in(key, 1), -6.0, 6.0, (FRAMES, DT), jnp.float32)
    return drawn.astype(jnp.bfloat16)


def draw_w_proj(key, part):
    spread = DT ** (-0.5)
    drawn = jax.random.truncated_normal(jax.random.fold_in(key, 11), -6.0, 6.0, (DT, DD), jnp.float32) * spread
    return drawn.astype(jnp.bfloat16)


def draw_w_qkv(key, part):
    spread = DD ** (-0.5)
    drawn = jax.random.truncated_normal(jax.random.fold_in(key, 21), -6.0, 6.0, (DD, 3, DD), jnp.float32) * spread
    return drawn.astype(jnp.bfloat16)


def draw_head_table(key, part):
    spread = (DD // 9) ** (-0.5)
    drawn = jax.random.truncated_normal(jax.random.fold_in(key, 31), -6.0, 6.0, (KW, DD, V), jnp.float32) * spread
    return drawn.astype(jnp.bfloat16)


def plant(values, key, smallest, top_value):
    place = [jax.random.randint(jax.random.fold_in(key, axis), (), 0, length) for axis, length in enumerate(values.shape)]
    longest = values.shape.index(max(values.shape))
    beside = place[:longest] + [(place[longest] + 1) % values.shape[longest]] + place[longest + 1:]
    return values.at[tuple(place)].set(smallest).at[tuple(beside)].set(top_value)


def block_scale(own_key, extent, pieces, smallest, largest):
    factor_of = 1.0
    for dim, blocks in pieces:
        steps = jax.random.uniform(jax.random.fold_in(jax.random.fold_in(own_key, 6), dim), (blocks,), jnp.float32, smallest / len(pieces), largest / len(pieces))
        factor_of = factor_of * jnp.repeat(jnp.exp(steps), extent[dim] // blocks).reshape((-1,) + (1,) * (len(extent) - 1 - dim))
    return factor_of


def bell_draw(rng, shape, deviation, most, pieces=(), held_as=jnp.bfloat16):
    entries = jax.random.normal(rng, shape, jnp.float32) * deviation
    if len(pieces) > 0:
        entries = block_scale(rng, shape, pieces, -0.22, 0.18) * entries
    return jnp.clip(entries, min=-most, max=most).astype(held_as)


def setup_inputs(seed: int = 0) -> dict:
    splits = jax.random.split(jax.random.key(seed), 10)
    return {
        "hidden": draw_hidden(jax.random.fold_in(splits[9], 71), 0),
        "w_proj": draw_w_proj(jax.random.fold_in(splits[9], 71), 0),
        "codes": plant(jax.random.randint(splits[2], (FRAMES, KW), 0, V), jax.random.fold_in(splits[2], 1), 0, V - 1).astype(jnp.int32),
        "embed_table": bell_draw(splits[3], (KW - 1, V, DD), 1.0, 6.0, ((2, 4),)),
        "w_qkv": draw_w_qkv(jax.random.fold_in(splits[9], 71), 0),
        "w_out": bell_draw(splits[5], (DD, DD), DD ** -0.5, 0.1875, ((0, 4),)),
        "head_table": draw_head_table(jax.random.fold_in(splits[9], 71), 0),
        "gain_attn": jnp.clip(1.0 + 0.1 * jax.random.normal(splits[7], (DD,), jnp.float32), 0.5, 1.5),
        "gain_head": jnp.clip(1.0 + 0.1 * jax.random.normal(splits[8], (DD,), jnp.float32), 0.5, 1.5),
    }


def rms_norm(stream, gain):
    return stream * lax.rsqrt(lax.optimization_barrier(jnp.mean(stream * stream, axis=-1, keepdims=True)) + 1e-06) * gain

def norm_back(stream, gain, cotangent):
    return jax.vjp(lambda value: rms_norm(value, gain), stream)[1](cotangent)[0]

def attend(query, keys, values):
    scale = query.shape[-1] ** (-0.5)
    count = query.shape[1]
    scores = jnp.einsum('fqhd,fkhd->fhqk', query.astype(jnp.float32), keys.astype(jnp.float32)) * scale
    causal = jnp.arange(count)[:, None] >= jnp.arange(count)[None, :]
    scores = jnp.where(causal, scores, -1e+30)
    shifted = jnp.exp(scores - lax.optimization_barrier(jnp.max(scores, axis=-1, keepdims=True)))
    weights = shifted / lax.optimization_barrier(jnp.sum(shifted, axis=-1, keepdims=True))
    weights_low = weights.astype(jnp.bfloat16)
    attended = jnp.einsum('fhqk,fkhd->fqhd', weights_low.astype(jnp.float32), values.astype(jnp.float32)).astype(jnp.bfloat16)
    return (attended, weights, weights_low)

def attend_back(query, keys, values, weights, weights_low, attended_grad):
    scale = query.shape[-1] ** (-0.5)
    grad_f = attended_grad.astype(jnp.float32)
    prob_grad = jnp.einsum('fqhd,fkhd->fhqk', grad_f, values.astype(jnp.float32))
    score_grad = (weights * (prob_grad - lax.optimization_barrier(jnp.sum(weights * prob_grad, axis=-1, keepdims=True))) * scale).astype(jnp.bfloat16)
    score_f = score_grad.astype(jnp.float32)
    query_grad = jnp.einsum('fhqk,fkhd->fqhd', score_f, keys.astype(jnp.float32)).astype(jnp.bfloat16)
    key_grad = jnp.einsum('fhqk,fqhd->fkhd', score_f, query.astype(jnp.float32)).astype(jnp.bfloat16)
    value_grad = jnp.einsum('fhqk,fqhd->fkhd', weights_low.astype(jnp.float32), grad_f).astype(jnp.bfloat16)
    return jnp.stack([query_grad, key_grad, value_grad], axis=2)

def reference(hidden, w_proj, codes, embed_table, w_qkv, w_out, head_table, gain_attn, gain_head):
    frames = hidden.shape[0]
    width = w_proj.shape[1]
    head_dim = width // HEADS
    total = float(frames * KW)
    context = jnp.dot(hidden, w_proj, preferred_element_type=jnp.float32)
    looked = jnp.stack([jnp.take(embed_table[column], codes[:, column], axis=0) for column in range(KW - 1)], axis=1)
    shifted_in = jnp.concatenate([jnp.zeros((frames, 1, width), jnp.float32), looked.astype(jnp.float32)], axis=1)
    stream_in = context[:, None, :] + shifted_in
    normed_in = rms_norm(stream_in, gain_attn).astype(jnp.bfloat16)
    projected = jnp.dot(normed_in.reshape(-1, width), w_qkv.reshape(width, -1), preferred_element_type=jnp.float32)
    projected = projected.astype(jnp.bfloat16).reshape(frames, KW, 3, HEADS, head_dim)
    query, keys, values = (projected[:, :, 0], projected[:, :, 1], projected[:, :, 2])
    attended, weights, weights_low = attend(query, keys, values)
    mixed = jnp.dot(attended.reshape(-1, width), w_out, preferred_element_type=jnp.float32)
    stream_mid = stream_in + mixed.reshape(frames, KW, width)
    normed_out = rms_norm(stream_mid, gain_head).astype(jnp.bfloat16)
    logits = jnp.einsum('fkd,kdv->fkv', normed_out.astype(jnp.float32), head_table.astype(jnp.float32))
    hits = codes[..., None] == jnp.arange(logits.shape[-1], dtype=jnp.int32)
    top = lax.optimization_barrier(jnp.max(logits, axis=-1))
    exp_total = lax.optimization_barrier(jnp.sum(jnp.exp(logits - top[..., None]), axis=-1))
    log_total = top + jnp.log(exp_total)
    target = lax.optimization_barrier(jnp.sum(jnp.where(hits, logits, 0.0), axis=-1))
    row_loss = log_total - target
    logit_grad = ((jnp.exp(logits - log_total[..., None]) - hits.astype(jnp.float32)) / total).astype(jnp.bfloat16)
    normed_grad = jnp.einsum('fkv,kdv->fkd', logit_grad.astype(jnp.float32), head_table.astype(jnp.float32))
    mid_grad = norm_back(stream_mid, gain_head, normed_grad)
    mid_low = mid_grad.astype(jnp.bfloat16)
    attended_grad = jnp.dot(mid_low.reshape(-1, width), w_out.T, preferred_element_type=jnp.float32)
    attended_grad = attended_grad.astype(jnp.bfloat16).reshape(frames, KW, HEADS, head_dim)
    qkv_grad = attend_back(query, keys, values, weights, weights_low, attended_grad)
    normin_grad = jnp.dot(qkv_grad.reshape(frames * KW, -1), w_qkv.reshape(width, -1).T, preferred_element_type=jnp.float32)
    stream_grad = mid_grad + norm_back(stream_in, gain_attn, normin_grad.reshape(frames, KW, width))
    context_grad = lax.optimization_barrier(jnp.sum(stream_grad, axis=1)).astype(jnp.bfloat16)
    grad_hidden = jnp.dot(context_grad, w_proj.T, preferred_element_type=jnp.float32).astype(jnp.bfloat16)
    grad_proj = jnp.dot(hidden.T, context_grad, preferred_element_type=jnp.float32)
    return (row_loss, grad_hidden, grad_proj)
```

```python
import jax
import jax.numpy as jnp
from jax import lax
from jax.sharding import PartitionSpec as P

HEADS = 16
EPS = 1e-06
F32 = jnp.float32
BF16 = jnp.bfloat16


def dot(a, b):
    return lax.dot_general(a, b, (((1,), (0,)), ((), ())), preferred_element_type=F32)


def dot_t(a, b):
    return lax.dot_general(a, b, (((1,), (1,)), ((), ())), preferred_element_type=F32)


def inverse_rms(stream):
    return lax.rsqrt(jnp.mean(stream * stream, axis=-1, keepdims=True) + EPS)


def norm_back(stream, inverse, gain, cotangent):
    scaled = gain * cotangent
    along = jnp.mean(stream * scaled, axis=-1, keepdims=True)
    return inverse * scaled - stream * (inverse * inverse * inverse * along)


def head_sum(values, head_dim):
    lanes = values.shape[-1]
    rows = lax.broadcasted_iota(jnp.int32, (lanes, lanes), 0) // head_dim
    columns = lax.broadcasted_iota(jnp.int32, (lanes, lanes), 1) // head_dim
    return dot(values, jnp.where(rows == columns, 1.0, 0.0).astype(BF16))


def pairs_of(steps):
    return [(a, b) for a in range(steps) for b in range(a + 1)]


def attend(query, keys, values, head_dim):
    steps = len(query)
    count = query[0].shape[0]
    pairs = pairs_of(steps)
    products = jnp.concatenate([query[a] * keys[b] for a, b in pairs], axis=0)
    scores = head_sum(products, head_dim) * head_dim ** (-0.5)
    weights, attended = [], []
    for a in range(steps):
        first = pairs.index((a, 0))
        row = [scores[(first + b) * count : (first + b + 1) * count] for b in range(a + 1)]
        top = row[0]
        for item in row[1:]:
            top = jnp.maximum(top, item)
        row = [jnp.exp(item - top) for item in row]
        total = row[0]
        for item in row[1:]:
            total = total + item
        row = [item / total for item in row]
        mixed = 0.0
        for b in range(a + 1):
            mixed = mixed + row[b].astype(BF16).astype(F32) * values[b].astype(F32)
        weights += row
        attended.append(mixed.astype(BF16))
    return attended, weights


def attend_back(query, keys, values, weights, grads, head_dim):
    steps = len(query)
    count = query[0].shape[0]
    pairs = pairs_of(steps)
    scale = head_dim ** (-0.5)
    products = jnp.concatenate([grads[a] * values[b] for a, b in pairs], axis=0)
    probs = head_sum(products, head_dim)
    query_grad = [0.0] * steps
    key_grad = [0.0] * steps
    value_grad = [0.0] * steps
    for a in range(steps):
        first = pairs.index((a, 0))
        row = [probs[(first + b) * count : (first + b + 1) * count] for b in range(a + 1)]
        inner = 0.0
        for b in range(a + 1):
            inner = inner + weights[first + b] * row[b]
        for b in range(a + 1):
            weight = weights[first + b]
            score = (weight * (row[b] - inner) * scale).astype(BF16).astype(F32)
            query_grad[a] = query_grad[a] + score * keys[b].astype(F32)
            key_grad[b] = key_grad[b] + score * query[a].astype(F32)
            value_grad[b] = value_grad[b] + weight.astype(BF16).astype(F32) * grads[a].astype(F32)
    stack = lambda items: jnp.concatenate([item.astype(BF16) for item in items], axis=0)
    return stack(query_grad), stack(key_grad), stack(value_grad)


def split_rows(values, steps):
    count = values.shape[0] // steps
    return [values[k * count : (k + 1) * count] for k in range(steps)]


def seq_radices(size):
    radices = []
    while size % 4 == 0:
        radices.append(4)
        size //= 4
    return [size] + radices if size > 1 else radices


def body(hidden, w_proj, codes, embed_table, w_qkv, w_out, head_table, gain_attn, gain_head):
    frames, steps = codes.shape
    half = frames // 2
    width = w_proj.shape[1]
    head_dim = width // HEADS
    vocab = embed_table.shape[1]
    vocab_local = head_table.shape[2]
    tp = lax.axis_size("tp")
    seq = lax.axis_size("seq")
    total = float(frames * seq * steps)
    rank = lax.axis_index("tp")
    core = rank % 2
    side = rank // 2

    def to_core(value):
        return lax.ppermute(value, "tp", [(i, i ^ 1) for i in range(tp)])

    def to_side(value):
        return lax.ppermute(value, "tp", [(i, i ^ 2) for i in range(tp)])

    def rows_of(value, which, axis):
        return lax.dynamic_slice_in_dim(value, which * half, half, axis=axis)

    def ordered(flag, mine, theirs, axis):
        low = jnp.where(flag == 0, mine, theirs)
        high = jnp.where(flag == 0, theirs, mine)
        return jnp.concatenate([low, high], axis=axis)

    qkv_mine = w_qkv.reshape(width, -1)
    qkv_pair = to_core(qkv_mine)
    head_pair = to_core(head_table)
    out_side = to_side(w_out)
    out_mine = jnp.concatenate([w_out, to_core(w_out)], axis=0)
    out_theirs = jnp.concatenate([out_side, to_core(out_side)], axis=0)

    previous = codes[:, : steps - 1].T
    selector = (previous[..., None] == jnp.arange(vocab, dtype=jnp.int32)).astype(BF16)
    looked = jnp.einsum("kfv,kvd->kfd", selector, embed_table, preferred_element_type=F32).astype(BF16)
    looked = ordered(core, rows_of(looked, core, 1), to_core(rows_of(looked, 1 - core, 1)), 2)
    looked = ordered(side, looked, to_side(looked), 2).astype(F32)
    partial = dot(hidden, w_proj)
    partial = rows_of(partial, core, 0) + to_core(rows_of(partial, 1 - core, 0).astype(BF16)).astype(F32)
    partial = partial.astype(BF16)
    context = partial.astype(F32) + to_side(partial).astype(F32)
    my_codes = rows_of(codes, core, 0)

    stream_in = [context] + [context + looked[k] for k in range(steps - 1)]
    inverse_in = [inverse_rms(item) for item in stream_in]
    normed_in = jnp.concatenate(
        [(item * inv * gain_attn).astype(BF16) for item, inv in zip(stream_in, inverse_in)], axis=0
    )
    groups = []
    for weight in (qkv_mine, qkv_pair):
        projected = dot(normed_in, weight).astype(BF16)
        lanes = weight.shape[1] // 3
        parts = [split_rows(projected[:, j * lanes : (j + 1) * lanes], steps) for j in range(3)]
        attended, weights = attend(*parts, head_dim)
        groups.append((parts, weights, jnp.concatenate(attended, axis=0)))
    att_mine = jnp.concatenate([group[2] for group in groups], axis=1)
    att_theirs = to_side(att_mine)

    mixed = dot(att_mine, out_mine) + dot(att_theirs, out_theirs)
    stream_mid = [a + b for a, b in zip(stream_in, split_rows(mixed, steps))]
    inverse_mid = [inverse_rms(item) for item in stream_mid]
    lanes = lax.broadcasted_iota(jnp.int32, (half, vocab_local), 1)
    stats, numerators = [], []
    for k in range(steps):
        normed = (stream_mid[k] * inverse_mid[k] * gain_head).astype(BF16)
        code = my_codes[:, k : k + 1]
        tables = (head_table[k], head_pair[k])
        logits = [dot(normed, table) for table in tables]
        hits = [lanes == code - (rank ^ j) * vocab_local for j in range(2)]
        top = jnp.maximum(*[jnp.max(item, axis=-1, keepdims=True) for item in logits])
        exps = [jnp.exp(item - top) for item in logits]
        exp_sum = sum(jnp.sum(item, axis=-1, keepdims=True) for item in exps)
        target = sum(jnp.sum(jnp.where(h, l, 0.0), axis=-1, keepdims=True) for h, l in zip(hits, logits))
        stats += [top, exp_sum, target]
        numerators.append(
            [
                jnp.concatenate([jnp.where(h, 0.0, e).astype(BF16), h.astype(BF16)], axis=0)
                for h, e in zip(hits, exps)
            ]
        )
    stats = jnp.concatenate(stats, axis=1)
    stats_theirs = to_side(stats)
    losses, mid_grad = [], []
    for k in range(steps):
        both = dot_t(numerators[k][0], head_table[k]) + dot_t(numerators[k][1], head_pair[k])
        top_a, sum_a, target_a = [stats[:, 3 * k + j : 3 * k + j + 1] for j in range(3)]
        top_b, sum_b, target_b = [stats_theirs[:, 3 * k + j : 3 * k + j + 1] for j in range(3)]
        top = jnp.maximum(top_a, top_b)
        log_total = top + jnp.log(sum_a * jnp.exp(top_a - top) + sum_b * jnp.exp(top_b - top))
        target = target_a + target_b
        losses.append(log_total - target)
        part = both[:half] * (jnp.exp(top_a - log_total) / total)
        part = part + both[half:] * ((jnp.exp(target - log_total) - 1.0) / total)
        mid_grad.append(norm_back(stream_mid[k], inverse_mid[k], gain_head, part))
    mid_low = jnp.concatenate([item.astype(BF16) for item in mid_grad], axis=0)
    att_grad_out = dot_t(mid_low, out_theirs).astype(BF16)
    att_grad = (dot_t(mid_low, out_mine) + to_side(att_grad_out).astype(F32)).astype(BF16)

    normin = 0.0
    lanes = att_grad.shape[1] // 2
    for j, weight in enumerate((qkv_mine, qkv_pair)):
        parts, weights, _ = groups[j]
        grads = split_rows(att_grad[:, j * lanes : (j + 1) * lanes], steps)
        grads = attend_back(*parts, weights, grads, head_dim)
        normin = normin + dot_t(jnp.concatenate(grads, axis=1), weight)
    part = 0.0
    for k, item in enumerate(split_rows(normin, steps)):
        part = part + mid_grad[k] + norm_back(stream_in[k], inverse_in[k], gain_attn, item)
    part = part.astype(BF16)
    context_grad = (part.astype(F32) + to_side(part).astype(F32)).astype(BF16)

    losses = jnp.concatenate(losses, axis=1)
    row_loss = ordered(core, losses, to_core(losses), 0)
    full_grad = ordered(core, context_grad, to_core(context_grad), 0)
    grad_hidden = dot_t(full_grad, w_proj).astype(BF16)

    index = lax.axis_index("seq")
    owned = context_grad.reshape(1, half, seq, width // seq)
    states = [hidden[None]]
    low = 1
    for radix in seq_radices(seq):
        rows = jnp.concatenate(states, axis=0)
        digit = (index // low) % radix
        blocks = owned.reshape(owned.shape[0], half, owned.shape[2] // radix, radix, -1)
        keep, states = [], []
        for shift in range(radix):
            pick = lax.dynamic_index_in_dim(blocks, (digit + shift) % radix, axis=3, keepdims=False)
            if shift == 0:
                keep.append(pick)
                states.append(rows)
                continue
            route = []
            for i in range(seq):
                d = (i // low) % radix
                route.append((i, i + ((d + shift) % radix - d) * low))
            keep.append(lax.ppermute(pick, "seq", route))
            states.append(lax.ppermute(rows, "seq", route))
        owned = jnp.concatenate(keep, axis=0)
        low *= radix
    owned = owned.reshape(seq, half, -1)
    owned = ordered(core, owned, to_core(owned), 1).reshape(len(states), -1, owned.shape[2])
    grad_proj = 0.0
    for rows, grads in zip(states, owned):
        grad_proj = grad_proj + lax.dot_general(
            rows.reshape(grads.shape[0], -1), grads, (((0,), (0,)), ((), ())), preferred_element_type=F32
        )
    return (row_loss, grad_hidden, grad_proj)


def solution(mesh):
    return jax.shard_map(
        body,
        mesh=mesh,
        in_specs=(
            P("seq", "tp"),
            P("tp", None),
            P("seq", None),
            P(None, None, "tp"),
            P(None, None, "tp"),
            P("tp", None),
            P(None, None, "tp"),
            P(),
            P(),
        ),
        out_specs=(P("seq", None), P("seq", "tp"), P("tp", "seq")),
        check_vma=False,
    )
```

```python
import functools

import jax
import jax.numpy as jnp
from jax import lax
from jax.experimental import pallas as pl
from jax.experimental.pallas import tpu as pltpu
from jax.sharding import PartitionSpec as P

HEADS = 16
EPS = 1e-06
ROWS = 16
F32 = jnp.float32
BF16 = jnp.bfloat16
VMEM_BYTES = 28 * 1024 * 1024


def dot(a, b):
    return lax.dot_general(a, b, (((1,), (0,)), ((), ())), preferred_element_type=F32)


def dot_t(a, b):
    return lax.dot_general(a, b, (((1,), (1,)), ((), ())), preferred_element_type=F32)


def inverse_rms(stream):
    return lax.rsqrt(jnp.mean(stream * stream, axis=-1, keepdims=True) + EPS)


def norm_back(stream, gain, cotangent):
    inverse = inverse_rms(stream)
    scaled = gain * cotangent
    along = jnp.mean(stream * scaled, axis=-1, keepdims=True)
    return inverse * scaled - stream * (inverse * inverse * inverse * along)


def head_ones(lanes, head_dim):
    rows = lax.broadcasted_iota(jnp.int32, (lanes, lanes), 0) // head_dim
    columns = lax.broadcasted_iota(jnp.int32, (lanes, lanes), 1) // head_dim
    return jnp.where(rows == columns, 1.0, 0.0).astype(BF16)


def pairs_of(steps):
    return [(a, b) for a in range(steps) for b in range(a + 1)]


def call(kernel, name, outs, scratch, args, cost, spaces=None):
    specs = [pl.BlockSpec(memory_space=pltpu.VMEM) for _ in args]
    for place, space in (spaces or {}).items():
        specs[place] = pl.BlockSpec(memory_space=space)
    return pl.pallas_call(
        kernel,
        name=name,
        out_shape=[jax.ShapeDtypeStruct(shape, dtype) for shape, dtype in outs],
        in_specs=specs,
        out_specs=[pl.BlockSpec(memory_space=pltpu.VMEM) for _ in outs],
        scratch_shapes=scratch,
        cost_estimate=pl.CostEstimate(flops=cost, bytes_accessed=cost // 300, transcendentals=0),
        compiler_params=pltpu.CompilerParams(vmem_limit_bytes=VMEM_BYTES),
    )(*args)


def chunk(index):
    return pl.ds(pl.multiple_of(index * ROWS, ROWS), ROWS)


def at_row(base, index):
    return pl.ds(pl.multiple_of(base + index * ROWS, ROWS), ROWS)


def lookup_kernel(codes_ref, table_hbm, mine_ref, other_ref, table_ref, sems):
    count = mine_ref.shape[0]
    half = mine_ref.shape[1]
    vocab = table_ref.shape[1]
    core = lax.axis_index("tp") % 2
    copies = [
        pltpu.make_async_copy(table_hbm.at[k], table_ref.at[k], sems.at[k]) for k in range(count)
    ]
    for copy in copies:
        copy.start()
    low = codes_ref[pl.ds(pl.multiple_of(core * half, half), half), :]
    high = codes_ref[pl.ds(pl.multiple_of((1 - core) * half, half), half), :]
    codes = jnp.concatenate([low, high], axis=0)
    lanes = lax.broadcasted_iota(jnp.int32, (2 * half, vocab), 1)
    for k in range(count):
        chosen = jnp.where(lanes == codes[:, k : k + 1], 1.0, 0.0).astype(BF16)
        copies[k].wait()
        found = dot(chosen, table_ref[k]).astype(BF16)
        mine_ref[k] = found[:half]
        other_ref[k] = found[half:]


def context_kernel(hidden_ref, weight_ref, mine_ref, other_ref):
    half = mine_ref.shape[0]
    core = lax.axis_index("tp") % 2
    low = hidden_ref[pl.ds(pl.multiple_of(core * half, half), half), :]
    high = hidden_ref[pl.ds(pl.multiple_of((1 - core) * half, half), half), :]
    partial = dot(jnp.concatenate([low, high], axis=0), weight_ref[...])
    mine_ref[...] = partial[:half]
    other_ref[...] = partial[half:].astype(BF16)


def attention_kernel(
    head_dim, own_ref, side_ref, look0, look1, look2, look3, qkv_mine, qkv_pair, gain_ref,
    stream_ref, att_ref, proj_mine, proj_pair, soft_mine, soft_pair,
    look_ref, normed_ref, product_ref, score_ref,
):
    steps, half, width = stream_ref.shape
    rank = lax.axis_index("tp")
    lanes = look0.shape[2]
    chunks = half // ROWS
    pairs = pairs_of(steps)
    scale = head_dim ** (-0.5)
    for j, look in enumerate((look0, look1, look2, look3)):
        place = pl.ds(pl.multiple_of((rank ^ j) * lanes, lanes), lanes)
        for k in range(steps - 1):
            look_ref[k, :, place] = look[k]

    def enter(i, carry):
        context = own_ref[chunk(i), :].astype(F32) + side_ref[chunk(i), :].astype(F32)
        for k in range(steps):
            stream = context if k == 0 else context + look_ref[k - 1, chunk(i), :].astype(F32)
            stream_ref[k, chunk(i), :] = stream
            normed = stream * inverse_rms(stream) * gain_ref[...]
            normed_ref[at_row(k * half, i), :] = normed.astype(BF16)
        return carry

    lax.fori_loop(0, chunks, enter, 0)
    ones = head_ones(lanes, head_dim)
    for j, (weight, proj, soft) in enumerate(
        ((qkv_mine, proj_mine, soft_mine), (qkv_pair, proj_pair, soft_pair))
    ):
        proj[...] = dot(normed_ref[...], weight[...]).astype(BF16)

        def multiply(i, carry):
            rows = [at_row(k * half, i) for k in range(steps)]
            query = [proj[row, 0:lanes] for row in rows]
            keys = [proj[row, lanes : 2 * lanes] for row in rows]
            for p, (a, b) in enumerate(pairs):
                product_ref[at_row(p * half, i), :] = query[a] * keys[b]
            return carry

        lax.fori_loop(0, chunks, multiply, 0)
        score_ref[...] = dot(product_ref[...], ones) * scale

        def weigh(i, carry):
            rows = [at_row(k * half, i) for k in range(steps)]
            values = [proj[row, 2 * lanes : 3 * lanes].astype(F32) for row in rows]
            for a in range(steps):
                first = pairs.index((a, 0))
                row = [score_ref[at_row((first + b) * half, i), :] for b in range(a + 1)]
                top = functools.reduce(jnp.maximum, row)
                row = [jnp.exp(item - top) for item in row]
                total = functools.reduce(jnp.add, row)
                mixed = 0.0
                for b in range(a + 1):
                    weight_ab = row[b] / total
                    soft[at_row((first + b) * half, i), :] = weight_ab
                    mixed = mixed + weight_ab.astype(BF16).astype(F32) * values[b]
                att_ref[rows[a], j * lanes : (j + 1) * lanes] = mixed.astype(BF16)
            return carry

        lax.fori_loop(0, chunks, weigh, 0)


def head_kernel(
    att_mine, att_theirs, out_mine, out_theirs, stream_ref, gain_ref, codes_ref, head_mine, head_pair,
    mid_ref, expo_ref, stats_ref, mixed_ref, normed_ref, logit_ref,
):
    steps, half, width = stream_ref.shape
    rank = lax.axis_index("tp")
    core = rank % 2
    vocab = head_mine.shape[2]
    chunks = half // ROWS
    mixed_ref[...] = dot(att_mine[...], out_mine[...]) + dot(att_theirs[...], out_theirs[...])

    def enter(i, carry):
        for k in range(steps):
            stream = stream_ref[k, chunk(i), :] + mixed_ref[at_row(k * half, i), :]
            mid_ref[k, chunk(i), :] = stream
            normed = stream * inverse_rms(stream) * gain_ref[...]
            normed_ref[at_row(k * half, i), :] = normed.astype(BF16)
        return carry

    lax.fori_loop(0, chunks, enter, 0)
    for k in range(steps):
        normed = normed_ref[k * half : (k + 1) * half, :]
        logit_ref[k, :, 0:vocab] = dot(normed, head_mine[k])
        logit_ref[k, :, vocab : 2 * vocab] = dot(normed, head_pair[k])

    def leave(i, carry):
        lanes = lax.broadcasted_iota(jnp.int32, (ROWS, 2 * vocab), 1)
        ids = jnp.where(lanes < vocab, lanes + rank * vocab, lanes - vocab + (rank ^ 1) * vocab)
        spots = lax.broadcasted_iota(jnp.int32, (ROWS, stats_ref.shape[1]), 1)
        stats = jnp.zeros((ROWS, stats_ref.shape[1]), F32)
        codes = codes_ref[pl.ds(pl.multiple_of(core * half + i * ROWS, ROWS), ROWS), :]
        for k in range(steps):
            logits = logit_ref[k, chunk(i), :]
            hits = ids == codes[:, k : k + 1]
            top = jnp.max(logits, axis=-1, keepdims=True)
            expo = jnp.exp(logits - top)
            total = jnp.sum(expo, axis=-1, keepdims=True)
            target = jnp.sum(jnp.where(hits, logits, 0.0), axis=-1, keepdims=True)
            expo_ref[k, chunk(i), :] = jnp.where(hits, 0.0, expo).astype(BF16)
            expo_ref[k, at_row(half, i), :] = jnp.where(hits, 1.0, 0.0).astype(BF16)
            for j, value in enumerate((top, total, target)):
                stats = jnp.where(spots == 3 * k + j, value, stats)
        stats_ref[chunk(i), :] = stats
        return carry

    lax.fori_loop(0, chunks, leave, 0)


def head_back_kernel(expo_ref, head_mine, head_pair, both_ref):
    vocab = head_mine.shape[2]
    for k in range(both_ref.shape[0]):
        both_ref[k] = dot_t(expo_ref[k, :, 0:vocab], head_mine[k]) + dot_t(
            expo_ref[k, :, vocab : 2 * vocab], head_pair[k]
        )


def mid_kernel(
    frames_total, both_ref, mid_ref, gain_ref, stats_ref, stats_side, out_mine, out_theirs,
    send_ref, keep_ref, sum_ref, loss_ref, low_ref,
):
    steps, half, width = mid_ref.shape

    def leave(i, carry):
        mine = stats_ref[chunk(i), :]
        theirs = stats_side[chunk(i), :]
        spots = lax.broadcasted_iota(jnp.int32, (ROWS, steps), 1)
        losses = jnp.zeros((ROWS, steps), F32)
        added = 0.0
        for k in range(steps):
            top_a, sum_a, target_a = [mine[:, 3 * k + j : 3 * k + j + 1] for j in range(3)]
            top_b, sum_b, target_b = [theirs[:, 3 * k + j : 3 * k + j + 1] for j in range(3)]
            top = jnp.maximum(top_a, top_b)
            log_total = top + jnp.log(sum_a * jnp.exp(top_a - top) + sum_b * jnp.exp(top_b - top))
            target = target_a + target_b
            losses = jnp.where(spots == k, log_total - target, losses)
            part = both_ref[k, chunk(i), :] * (jnp.exp(top_a - log_total) / frames_total)
            hit = (jnp.exp(target - log_total) - 1.0) / frames_total
            part = part + both_ref[k, at_row(half, i), :] * hit
            grad = norm_back(mid_ref[k, chunk(i), :], gain_ref[...], part)
            low_ref[at_row(k * half, i), :] = grad.astype(BF16)
            added = added + grad
        sum_ref[chunk(i), :] = added
        loss_ref[chunk(i), :] = losses
        return carry

    lax.fori_loop(0, half // ROWS, leave, 0)
    send_ref[...] = dot_t(low_ref[...], out_theirs[...]).astype(BF16)
    keep_ref[...] = dot_t(low_ref[...], out_mine[...])


def attention_back_kernel(
    head_dim, keep_ref, recv_ref, proj_mine, proj_pair, soft_mine, soft_pair, qkv_mine, qkv_pair,
    stream_ref, gain_ref, sum_ref, part_ref, grad_ref, product_ref, prob_ref, back_mine, back_pair, normin_ref,
):
    steps, half, width = stream_ref.shape
    lanes = keep_ref.shape[1] // 2
    chunks = half // ROWS
    pairs = pairs_of(steps)
    scale = head_dim ** (-0.5)
    ones = head_ones(lanes, head_dim)
    for j, (proj, soft, back) in enumerate(
        ((proj_mine, soft_mine, back_mine), (proj_pair, soft_pair, back_pair))
    ):
        span = slice(j * lanes, (j + 1) * lanes)

        def multiply(i, carry):
            rows = [at_row(k * half, i) for k in range(steps)]
            values = [proj[row, 2 * lanes : 3 * lanes] for row in rows]
            for a in range(steps):
                grad = (keep_ref[rows[a], span] + recv_ref[rows[a], span].astype(F32)).astype(BF16)
                grad_ref[rows[a], :] = grad
                for b in range(a + 1):
                    product_ref[at_row(pairs.index((a, b)) * half, i), :] = grad * values[b]
            return carry

        lax.fori_loop(0, chunks, multiply, 0)
        prob_ref[...] = dot(product_ref[...], ones)

        def spread(i, carry):
            rows = [at_row(k * half, i) for k in range(steps)]
            query_grad = [0.0] * steps
            key_grad = [0.0] * steps
            value_grad = [0.0] * steps
            for a in range(steps):
                first = pairs.index((a, 0))
                weights = [soft[at_row((first + b) * half, i), :] for b in range(a + 1)]
                probs = [prob_ref[at_row((first + b) * half, i), :] for b in range(a + 1)]
                inner = functools.reduce(jnp.add, [w * p for w, p in zip(weights, probs)])
                grad = grad_ref[rows[a], :].astype(F32)
                query = proj[rows[a], 0:lanes].astype(F32)
                for b in range(a + 1):
                    score = (weights[b] * (probs[b] - inner) * scale).astype(BF16).astype(F32)
                    key = proj[rows[b], lanes : 2 * lanes].astype(F32)
                    query_grad[a] = query_grad[a] + score * key
                    key_grad[b] = key_grad[b] + score * query
                    value_grad[b] = value_grad[b] + weights[b].astype(BF16).astype(F32) * grad
            for k in range(steps):
                back[rows[k], 0:lanes] = query_grad[k].astype(BF16)
                back[rows[k], lanes : 2 * lanes] = key_grad[k].astype(BF16)
                back[rows[k], 2 * lanes : 3 * lanes] = value_grad[k].astype(BF16)
            return carry

        lax.fori_loop(0, chunks, spread, 0)
    normin_ref[...] = dot_t(back_mine[...], qkv_mine[...]) + dot_t(back_pair[...], qkv_pair[...])

    def leave(i, carry):
        part = sum_ref[chunk(i), :]
        for k in range(steps):
            part = part + norm_back(stream_ref[k, chunk(i), :], gain_ref[...], normin_ref[at_row(k * half, i), :])
        part_ref[chunk(i), :] = part.astype(BF16)
        return carry

    lax.fori_loop(0, chunks, leave, 0)


def project_kernel(*refs):
    count = len(refs) // 2
    total = 0.0
    for rows, grads in zip(refs[:count], refs[count : 2 * count]):
        total = total + lax.dot_general(
            grads[...], rows[...], (((0,), (0,)), ((), ())), preferred_element_type=F32
        )
    refs[-1][...] = total.T


def seq_radices(size):
    radices = []
    while size % 4 == 0:
        radices.append(4)
        size //= 4
    return [size] + radices if size > 1 else radices


def body(hidden, w_proj, codes, embed_table, w_qkv, w_out, head_table, gain_attn, gain_head):
    frames, steps = codes.shape
    half = frames // 2
    width = w_proj.shape[1]
    head_dim = width // HEADS
    vocab_local = head_table.shape[2]
    lanes = w_qkv.shape[2]
    tp = lax.axis_size("tp")
    seq = lax.axis_size("seq")
    total = float(frames * seq * steps)
    pairs = len(pairs_of(steps))
    rank = lax.axis_index("tp")
    core = rank % 2
    rows = steps * half
    gain_attn = gain_attn.reshape(1, width)
    gain_head = gain_head.reshape(1, width)

    def to_peer(value, flip):
        return lax.ppermute(value, "tp", [(i, i ^ flip) for i in range(tp)])

    def ordered(flag, mine, theirs, axis):
        low = jnp.where(flag == 0, mine, theirs)
        high = jnp.where(flag == 0, theirs, mine)
        return jnp.concatenate([low, high], axis=axis)

    looked, looked_other = call(
        lookup_kernel, "lookup",
        [((steps - 1, half, lanes), BF16)] * 2,
        [pltpu.VMEM(embed_table.shape, BF16), pltpu.SemaphoreType.DMA((steps - 1,))],
        (codes, embed_table), 2 * frames * embed_table.size, {1: pl.ANY},
    )
    looked = [looked, to_peer(looked_other, 1), to_peer(looked, 2), to_peer(looked_other, 3)]
    partial, partial_other = call(
        context_kernel, "context", [((half, width), F32), ((half, width), BF16)], [],
        (hidden, w_proj), 2 * frames * w_proj.size,
    )
    partial = (partial + to_peer(partial_other, 1).astype(F32)).astype(BF16)
    partial_side = to_peer(partial, 2)

    qkv_mine = w_qkv.reshape(width, -1)
    qkv_pair = to_peer(qkv_mine, 1)
    head_pair = to_peer(head_table, 1)
    out_side = to_peer(w_out, 2)
    out_mine = jnp.concatenate([w_out, to_peer(w_out, 1)], axis=0)
    out_theirs = jnp.concatenate([out_side, to_peer(out_side, 1)], axis=0)

    stream_in, att_mine, proj_mine, proj_pair, soft_mine, soft_pair = call(
        functools.partial(attention_kernel, head_dim), "attention",
        [((steps, half, width), F32), ((rows, 2 * lanes), BF16)]
        + [((rows, 3 * lanes), BF16)] * 2 + [((pairs * half, lanes), F32)] * 2,
        [
            pltpu.VMEM((steps - 1, half, width), BF16),
            pltpu.VMEM((rows, width), BF16),
            pltpu.VMEM((pairs * half, lanes), BF16),
            pltpu.VMEM((pairs * half, lanes), F32),
        ],
        (partial, partial_side, *looked, qkv_mine, qkv_pair, gain_attn), 4 * rows * qkv_mine.size,
    )
    att_theirs = to_peer(att_mine, 2)
    stream_mid, expo, stats = call(
        head_kernel, "head",
        [((steps, half, width), F32), ((steps, 2 * half, 2 * vocab_local), BF16), ((half, 128), F32)],
        [
            pltpu.VMEM((rows, width), F32),
            pltpu.VMEM((rows, width), BF16),
            pltpu.VMEM((steps, half, 2 * vocab_local), F32),
        ],
        (att_mine, att_theirs, out_mine, out_theirs, stream_in, gain_head, codes, head_table, head_pair),
        4 * half * head_table.size + 4 * rows * out_mine.size,
    )
    stats_side = to_peer(stats, 2)
    (both,) = call(
        head_back_kernel, "head_back", [((steps, 2 * half, width), F32)], [],
        (expo, head_table, head_pair), 8 * half * head_table.size,
    )
    att_send, att_keep, mid_sum, losses = call(
        functools.partial(mid_kernel, total), "mid",
        [((rows, 2 * lanes), BF16), ((rows, 2 * lanes), F32), ((half, width), F32), ((half, steps), F32)],
        [pltpu.VMEM((rows, width), BF16)],
        (both, stream_mid, gain_head, stats, stats_side, out_mine, out_theirs),
        4 * rows * out_mine.size,
    )
    att_recv = to_peer(att_send, 2)
    (part,) = call(
        functools.partial(attention_back_kernel, head_dim), "attention_back",
        [((half, width), BF16)],
        [
            pltpu.VMEM((rows, lanes), BF16),
            pltpu.VMEM((pairs * half, lanes), BF16),
            pltpu.VMEM((pairs * half, lanes), F32),
            pltpu.VMEM((rows, 3 * lanes), BF16),
            pltpu.VMEM((rows, 3 * lanes), BF16),
            pltpu.VMEM((rows, width), F32),
        ],
        (att_keep, att_recv, proj_mine, proj_pair, soft_mine, soft_pair, qkv_mine, qkv_pair,
         stream_in, gain_attn, mid_sum),
        4 * rows * qkv_mine.size,
    )
    context_grad = (part.astype(F32) + to_peer(part, 2).astype(F32)).astype(BF16)

    row_loss = ordered(core, losses, to_peer(losses, 1), 0)
    full_grad = ordered(core, context_grad, to_peer(context_grad, 1), 0)
    grad_hidden = dot_t(full_grad, w_proj).astype(BF16)

    index = lax.axis_index("seq")
    owned = context_grad.reshape(1, half, seq, width // seq)
    states = [hidden[None]]
    low = 1
    for radix in seq_radices(seq):
        gathered = jnp.concatenate(states, axis=0)
        digit = (index // low) % radix
        blocks = owned.reshape(owned.shape[0], half, owned.shape[2] // radix, radix, -1)
        keep, states = [], []
        for shift in range(radix):
            pick = lax.dynamic_index_in_dim(blocks, (digit + shift) % radix, axis=3, keepdims=False)
            if shift == 0:
                keep.append(pick)
                states.append(gathered)
                continue
            route = []
            for i in range(seq):
                d = (i // low) % radix
                route.append((i, i + ((d + shift) % radix - d) * low))
            keep.append(lax.ppermute(pick, "seq", route))
            states.append(lax.ppermute(gathered, "seq", route))
        owned = jnp.concatenate(keep, axis=0)
        low *= radix
    owned = owned.reshape(seq, half, -1)
    owned = ordered(core, owned, to_peer(owned, 1), 1).reshape(len(states), -1, owned.shape[2])
    grad_proj = 0.0
    for rows, grads in zip(states, owned):
        grad_proj = grad_proj + lax.dot_general(
            rows.reshape(grads.shape[0], -1), grads, (((0,), (0,)), ((), ())), preferred_element_type=F32
        )
    return (row_loss, grad_hidden, grad_proj)


def solution(mesh):
    return jax.shard_map(
        body,
        mesh=mesh,
        in_specs=(
            P("seq", "tp"),
            P("tp", None),
            P("seq", None),
            P(None, None, "tp"),
            P(None, None, "tp"),
            P("tp", None),
            P(None, None, "tp"),
            P(),
            P(),
        ),
        out_specs=(P("seq", None), P("seq", "tp"), P("tp", "seq")),
        check_vma=False,
    )
```

```python
import functools

import jax
import jax.numpy as jnp
from jax import lax
from jax.experimental import pallas as pl
from jax.experimental.pallas import tpu as pltpu
from jax.sharding import PartitionSpec as P


HEADS = 16
EPS = 1e-06
ROWS = 16
F32 = jnp.float32
BF16 = jnp.bfloat16


def dot(a, b):
    return lax.dot_general(a, b, (((1,), (0,)), ((), ())), preferred_element_type=F32)


def dot_t(a, b):
    return lax.dot_general(a, b, (((1,), (1,)), ((), ())), preferred_element_type=F32)


def inverse_rms(stream):
    return lax.rsqrt(jnp.mean(stream * stream, axis=-1, keepdims=True) + EPS)


def norm_back(stream, gain, cotangent):
    inverse = inverse_rms(stream)
    scaled = gain * cotangent
    along = jnp.mean(stream * scaled, axis=-1, keepdims=True)
    return inverse * scaled - stream * (inverse * inverse * inverse * along)


def head_ones(lanes, head_dim):
    rows = lax.broadcasted_iota(jnp.int32, (lanes, lanes), 0) // head_dim
    columns = lax.broadcasted_iota(jnp.int32, (lanes, lanes), 1) // head_dim
    return jnp.where(rows == columns, 1.0, 0.0).astype(BF16)


def pairs_of(steps):
    return [(a, b) for a in range(steps) for b in range(a + 1)]


def call(kernel, outs, scratch, args, cost, spaces=None, limit=16):
    specs = [pl.BlockSpec(memory_space=pltpu.VMEM) for _ in args]
    for place, space in (spaces or {}).items():
        specs[place] = pl.BlockSpec(memory_space=space)
    return pl.pallas_call(
        kernel,
        out_shape=[jax.ShapeDtypeStruct(shape, dtype) for shape, dtype in outs],
        in_specs=specs,
        out_specs=[pl.BlockSpec(memory_space=pltpu.VMEM) for _ in outs],
        scratch_shapes=scratch,
        cost_estimate=pl.CostEstimate(flops=cost, bytes_accessed=cost // 300, transcendentals=0),
        compiler_params=pltpu.CompilerParams(vmem_limit_bytes=limit * 1024 * 1024),
    )(*args)


def chunk(index):
    return pl.ds(pl.multiple_of(index * ROWS, ROWS), ROWS)


def at_row(base, index):
    return pl.ds(pl.multiple_of(base + index * ROWS, ROWS), ROWS)


def cut_kernel(weight_ref, out_ref):
    rows = out_ref.shape[0]
    place = lax.axis_index("seq") % 2 * rows
    out_ref[...] = weight_ref[pl.ds(pl.multiple_of(place, rows), rows), :]


def lookup_kernel(codes_ref, table_ref, mine_ref, other_ref):
    count, half = mine_ref.shape[:2]
    vocab = table_ref.shape[1]
    core = lax.axis_index("tp") % 2
    low = codes_ref[pl.ds(pl.multiple_of(core * half, half), half), :]
    high = codes_ref[pl.ds(pl.multiple_of((1 - core) * half, half), half), :]
    codes = jnp.concatenate([low, high], axis=0)
    lanes = lax.broadcasted_iota(jnp.int32, (2 * half, vocab), 1)
    for k in range(count):
        chosen = jnp.where(lanes == codes[:, k : k + 1], 1.0, 0.0).astype(BF16)
        found = dot(chosen, table_ref[k]).astype(BF16)
        mine_ref[k] = found[:half]
        other_ref[k] = found[half:]


def context_kernel(hidden_ref, weight_ref, mine_ref, other_ref):
    half = mine_ref.shape[0]
    core = lax.axis_index("tp") % 2
    low = hidden_ref[pl.ds(pl.multiple_of(core * half, half), half), :]
    high = hidden_ref[pl.ds(pl.multiple_of((1 - core) * half, half), half), :]
    partial = dot(jnp.concatenate([low, high], axis=0), weight_ref[...])
    mine_ref[...] = partial[:half]
    other_ref[...] = partial[half:].astype(BF16)


def attention_kernel(
    head_dim, own_ref, side_ref, look0, look1, look2, look3, qkv_mine, qkv_pair, gain_ref,
    stream_ref, att_ref, proj_mine, proj_pair, soft_mine, soft_pair,
    look_ref, normed_ref, product_ref, score_ref,
):
    steps, half, _ = stream_ref.shape
    rank = lax.axis_index("tp")
    lanes = look0.shape[2]
    chunks = half // ROWS
    pairs = pairs_of(steps)
    scale = head_dim ** (-0.5)
    for j, look in enumerate((look0, look1, look2, look3)):
        place = pl.ds(pl.multiple_of((rank ^ j) * lanes, lanes), lanes)
        for k in range(steps - 1):
            look_ref[k, :, place] = look[k]

    def enter(i, carry):
        context = own_ref[chunk(i), :].astype(F32) + side_ref[chunk(i), :].astype(F32)
        for k in range(steps):
            stream = context if k == 0 else context + look_ref[k - 1, chunk(i), :].astype(F32)
            stream_ref[k, chunk(i), :] = stream
            normed = stream * inverse_rms(stream) * gain_ref[...]
            normed_ref[at_row(k * half, i), :] = normed.astype(BF16)
        return carry

    lax.fori_loop(0, chunks, enter, 0)
    ones = head_ones(lanes, head_dim)
    for j, (weight, proj, soft) in enumerate(
        ((qkv_mine, proj_mine, soft_mine), (qkv_pair, proj_pair, soft_pair))
    ):
        for part in range(3):
            proj[:, part * lanes : (part + 1) * lanes] = dot(normed_ref[...], weight[part]).astype(BF16)

        def multiply(i, carry):
            rows = [at_row(k * half, i) for k in range(steps)]
            query = [proj[row, 0:lanes] for row in rows]
            keys = [proj[row, lanes : 2 * lanes] for row in rows]
            for p, (a, b) in enumerate(pairs):
                product_ref[at_row(p * half, i), :] = query[a] * keys[b]
            return carry

        lax.fori_loop(0, chunks, multiply, 0)
        score_ref[...] = dot(product_ref[...], ones) * scale

        def weigh(i, carry):
            rows = [at_row(k * half, i) for k in range(steps)]
            values = [proj[row, 2 * lanes : 3 * lanes].astype(F32) for row in rows]
            for a in range(steps):
                first = pairs.index((a, 0))
                row = [score_ref[at_row((first + b) * half, i), :] for b in range(a + 1)]
                top = functools.reduce(jnp.maximum, row)
                row = [jnp.exp(item - top) for item in row]
                total = functools.reduce(jnp.add, row)
                mixed = 0.0
                for b in range(a + 1):
                    weight_ab = row[b] / total
                    soft[at_row((first + b) * half, i), :] = weight_ab
                    mixed = mixed + weight_ab.astype(BF16).astype(F32) * values[b]
                att_ref[rows[a], j * lanes : (j + 1) * lanes] = mixed.astype(BF16)
            return carry

        lax.fori_loop(0, chunks, weigh, 0)


def head_kernel(
    att_mine, att_theirs, own_ref, pair_ref, part_a, part_b, part_c, part_d, stream_ref, gain_ref, codes_ref, head_mine, head_pair,
    mid_ref, expo_ref, stats_ref, full_ref, mixed_ref, normed_ref, logit_ref,
):
    steps, half, _ = stream_ref.shape
    rank = lax.axis_index("tp")
    core = rank % 2
    vocab = head_mine.shape[2]
    chunks = half // ROWS
    lanes, cut = own_ref.shape[0], part_a.shape[0]
    place = lax.axis_index("seq") % 2
    full_ref[0:lanes, :] = own_ref[...]
    full_ref[lanes : 2 * lanes, :] = pair_ref[...]
    for base, first, second in ((2 * lanes, part_a, part_b), (3 * lanes, part_c, part_d)):
        full_ref[pl.ds(pl.multiple_of(base + place * cut, cut), cut), :] = first[...]
        full_ref[pl.ds(pl.multiple_of(base + (1 - place) * cut, cut), cut), :] = second[...]
    mixed_ref[...] = dot(att_mine[...], full_ref[0 : 2 * lanes, :]) + dot(
        att_theirs[...], full_ref[2 * lanes : 4 * lanes, :]
    )

    def enter(i, carry):
        for k in range(steps):
            stream = stream_ref[k, chunk(i), :] + mixed_ref[at_row(k * half, i), :]
            mid_ref[k, chunk(i), :] = stream
            normed = stream * inverse_rms(stream) * gain_ref[...]
            normed_ref[at_row(k * half, i), :] = normed.astype(BF16)
        return carry

    lax.fori_loop(0, chunks, enter, 0)
    for k in range(steps):
        normed = normed_ref[k * half : (k + 1) * half, :]
        logit_ref[k, :, 0:vocab] = dot(normed, head_mine[k])
        logit_ref[k, :, vocab : 2 * vocab] = dot(normed, head_pair[k])

    def leave(i, carry):
        lanes = lax.broadcasted_iota(jnp.int32, (ROWS, 2 * vocab), 1)
        ids = jnp.where(lanes < vocab, lanes + rank * vocab, lanes - vocab + (rank ^ 1) * vocab)
        spots = lax.broadcasted_iota(jnp.int32, (ROWS, stats_ref.shape[1]), 1)
        stats = jnp.zeros((ROWS, stats_ref.shape[1]), F32)
        codes = codes_ref[pl.ds(pl.multiple_of(core * half + i * ROWS, ROWS), ROWS), :]
        for k in range(steps):
            logits = logit_ref[k, chunk(i), :]
            hits = ids == codes[:, k : k + 1]
            top = jnp.max(logits, axis=-1, keepdims=True)
            expo = jnp.exp(logits - top)
            total = jnp.sum(expo, axis=-1, keepdims=True)
            target = jnp.sum(jnp.where(hits, logits, 0.0), axis=-1, keepdims=True)
            expo_ref[k, chunk(i), :] = jnp.where(hits, 0.0, expo).astype(BF16)
            expo_ref[k, at_row(half, i), :] = jnp.where(hits, 1.0, 0.0).astype(BF16)
            for j, value in enumerate((top, total, target)):
                stats = jnp.where(spots == 3 * k + j, value, stats)
        stats_ref[chunk(i), :] = stats
        return carry

    lax.fori_loop(0, chunks, leave, 0)


def head_back_kernel(expo_ref, head_mine, head_pair, both_ref):
    vocab = head_mine.shape[2]
    for k in range(both_ref.shape[0]):
        both_ref[k] = dot_t(expo_ref[k, :, 0:vocab], head_mine[k]) + dot_t(
            expo_ref[k, :, vocab : 2 * vocab], head_pair[k]
        )


def mid_kernel(
    frames_total, both_ref, mid_ref, gain_ref, stats_ref, stats_side, out_ref,
    send_ref, keep_ref, sum_ref, loss_ref, low_ref,
):
    steps, half, _ = mid_ref.shape

    def leave(i, carry):
        mine = stats_ref[chunk(i), :]
        theirs = stats_side[chunk(i), :]
        spots = lax.broadcasted_iota(jnp.int32, (ROWS, steps), 1)
        losses = jnp.zeros((ROWS, steps), F32)
        added = 0.0
        for k in range(steps):
            top_a, sum_a, target_a = [mine[:, 3 * k + j : 3 * k + j + 1] for j in range(3)]
            top_b, sum_b, target_b = [theirs[:, 3 * k + j : 3 * k + j + 1] for j in range(3)]
            top = jnp.maximum(top_a, top_b)
            log_total = top + jnp.log(sum_a * jnp.exp(top_a - top) + sum_b * jnp.exp(top_b - top))
            target = target_a + target_b
            losses = jnp.where(spots == k, log_total - target, losses)
            part = both_ref[k, chunk(i), :] * (jnp.exp(top_a - log_total) / frames_total)
            hit = (jnp.exp(target - log_total) - 1.0) / frames_total
            part = part + both_ref[k, at_row(half, i), :] * hit
            grad = norm_back(mid_ref[k, chunk(i), :], gain_ref[...], part)
            low_ref[at_row(k * half, i), :] = grad.astype(BF16)
            added = added + grad
        sum_ref[chunk(i), :] = added
        loss_ref[chunk(i), :] = losses
        return carry

    lax.fori_loop(0, half // ROWS, leave, 0)
    middle = out_ref.shape[0] // 2
    send_ref[...] = dot_t(low_ref[...], out_ref[middle : 2 * middle, :]).astype(BF16)
    keep_ref[...] = dot_t(low_ref[...], out_ref[0:middle, :])


def attention_back_kernel(
    head_dim, keep_ref, recv_ref, proj_mine, proj_pair, soft_mine, soft_pair, qkv_mine, qkv_pair,
    stream_ref, gain_ref, sum_ref, part_ref, grad_ref, product_ref, prob_ref, back_mine, back_pair, normin_ref,
):
    steps, half, _ = stream_ref.shape
    lanes = keep_ref.shape[1] // 2
    chunks = half // ROWS
    pairs = pairs_of(steps)
    scale = head_dim ** (-0.5)
    ones = head_ones(lanes, head_dim)
    for j, (proj, soft, back) in enumerate(
        ((proj_mine, soft_mine, back_mine), (proj_pair, soft_pair, back_pair))
    ):
        span = slice(j * lanes, (j + 1) * lanes)

        def multiply(i, carry):
            rows = [at_row(k * half, i) for k in range(steps)]
            values = [proj[row, 2 * lanes : 3 * lanes] for row in rows]
            for a in range(steps):
                grad = (keep_ref[rows[a], span] + recv_ref[rows[a], span].astype(F32)).astype(BF16)
                grad_ref[rows[a], :] = grad
                for b in range(a + 1):
                    product_ref[at_row(pairs.index((a, b)) * half, i), :] = grad * values[b]
            return carry

        lax.fori_loop(0, chunks, multiply, 0)
        prob_ref[...] = dot(product_ref[...], ones)

        def spread(i, carry):
            rows = [at_row(k * half, i) for k in range(steps)]
            query_grad = [0.0] * steps
            key_grad = [0.0] * steps
            value_grad = [0.0] * steps
            for a in range(steps):
                first = pairs.index((a, 0))
                weights = [soft[at_row((first + b) * half, i), :] for b in range(a + 1)]
                probs = [prob_ref[at_row((first + b) * half, i), :] for b in range(a + 1)]
                inner = functools.reduce(jnp.add, [w * p for w, p in zip(weights, probs)])
                grad = grad_ref[rows[a], :].astype(F32)
                query = proj[rows[a], 0:lanes].astype(F32)
                for b in range(a + 1):
                    score = (weights[b] * (probs[b] - inner) * scale).astype(BF16).astype(F32)
                    key = proj[rows[b], lanes : 2 * lanes].astype(F32)
                    query_grad[a] = query_grad[a] + score * key
                    key_grad[b] = key_grad[b] + score * query
                    value_grad[b] = value_grad[b] + weights[b].astype(BF16).astype(F32) * grad
            for k in range(steps):
                back[rows[k], 0:lanes] = query_grad[k].astype(BF16)
                back[rows[k], lanes : 2 * lanes] = key_grad[k].astype(BF16)
                back[rows[k], 2 * lanes : 3 * lanes] = value_grad[k].astype(BF16)
            return carry

        lax.fori_loop(0, chunks, spread, 0)
    total = 0.0
    for back, weight in ((back_mine, qkv_mine), (back_pair, qkv_pair)):
        for part in range(3):
            total = total + dot_t(back[:, part * lanes : (part + 1) * lanes], weight[part])
    normin_ref[...] = total

    def leave(i, carry):
        part = sum_ref[chunk(i), :]
        for k in range(steps):
            part = part + norm_back(stream_ref[k, chunk(i), :], gain_ref[...], normin_ref[at_row(k * half, i), :])
        part_ref[chunk(i), :] = part.astype(BF16)
        return carry

    lax.fori_loop(0, chunks, leave, 0)


def sum_kernel(radix, low, part_ref, side_ref, grad_ref, *refs):
    outs, blocks_ref = refs[:radix], refs[radix]
    count, _, size = blocks_ref.shape
    digit = lax.axis_index("seq") // low % radix
    grad = (part_ref[...].astype(F32) + side_ref[...].astype(F32)).astype(BF16)
    grad_ref[...] = grad
    for j in range(count):
        blocks_ref[j] = grad[:, j * size : (j + 1) * size]
    for shift, out in enumerate(outs):
        for w in range(count // radix):
            out[0, w] = blocks_ref[w * radix + (digit + shift) % radix]


def pick_kernel(count, radix, low, *refs):
    digit = lax.axis_index("seq") // low % radix
    for shift, out in enumerate(refs[count:]):
        place = 0
        for item in refs[:count]:
            for q in range(item.shape[0]):
                for w in range(item.shape[1] // radix):
                    out[place, w] = item[q, w * radix + (digit + shift) % radix]
                place += 1


def hidden_grad_kernel(mine_ref, pair_ref, loss_mine, loss_pair, weight_ref, out_ref, loss_ref, full_ref):
    half = mine_ref.shape[0]
    core = lax.axis_index("tp") % 2
    low = pl.ds(pl.multiple_of(core * half, half), half)
    high = pl.ds(pl.multiple_of((1 - core) * half, half), half)
    full_ref[low, :] = mine_ref[...]
    full_ref[high, :] = pair_ref[...]
    loss_ref[low, :] = loss_mine[...]
    loss_ref[high, :] = loss_pair[...]
    out_ref[...] = dot_t(full_ref[...], weight_ref[...]).astype(BF16)


def project_kernel(count, *refs):
    states, mine, pair = refs[:count], refs[count : 2 * count], refs[2 * count : 3 * count]
    out_ref, grads_ref = refs[3 * count :]
    half = mine[0].shape[2]
    core = lax.axis_index("tp") % 2
    for p, (low, high) in enumerate(zip(mine, pair)):
        for q in range(low.shape[0]):
            base = 2 * q * half
            grads_ref[p, pl.ds(pl.multiple_of(base + core * half, half), half), :] = low[q, 0]
            grads_ref[p, pl.ds(pl.multiple_of(base + (1 - core) * half, half), half), :] = high[q, 0]
    total = 0.0
    for p, rows in enumerate(states):
        total = total + lax.dot_general(
            grads_ref[p], rows[...].reshape(-1, rows.shape[2]),
            (((0,), (0,)), ((), ())), preferred_element_type=F32,
        )
    out_ref[...] = total.T


def seq_radices(size):
    radices = []
    while size % 4 == 0:
        radices.append(4)
        size //= 4
    return [size] + radices if size > 1 else radices


def compute(hidden, w_proj, codes, embed_table, w_qkv, w_out, head_table, gain_attn, gain_head):
    frames, steps = codes.shape
    half = frames // 2
    width = w_proj.shape[1]
    head_dim = width // HEADS
    vocab_local = head_table.shape[2]
    lanes = w_qkv.shape[2]
    tp = lax.axis_size("tp")
    seq = lax.axis_size("seq")
    total = float(frames * seq * steps)
    pairs = len(pairs_of(steps))
    rows = steps * half
    gain_attn = gain_attn.reshape(1, width)
    gain_head = gain_head.reshape(1, width)

    def to_peer(value, flip):
        return lax.ppermute(value, "tp", [(i, i ^ flip) for i in range(tp)])

    def along(value, low, radix, shift):
        route = []
        for i in range(seq):
            digit = i // low % radix
            route.append((i, i + ((digit + shift) % radix - digit) * low))
        return lax.ppermute(value, "seq", route)

    cut = lanes // 2
    (out_part,) = call(cut_kernel, [((cut, width), BF16)], [], (w_out,), 6 * 10**9, limit=4)
    out_part = to_peer(out_part, 2)
    partial, partial_other = call(
        context_kernel, [((half, width), F32), ((half, width), BF16)], [],
        (hidden, w_proj), 6 * 10**9,
    )
    looked, looked_other = call(
        lookup_kernel,
        [((steps - 1, half, lanes), BF16)] * 2,
        [],
        (codes, embed_table), 2 * frames * embed_table.size,
    )
    partial = (partial + to_peer(partial_other, 1).astype(F32)).astype(BF16)
    partial_side = to_peer(partial, 2)
    looked = [looked, to_peer(looked_other, 1), to_peer(looked, 2), to_peer(looked_other, 3)]

    qkv_mine = w_qkv.transpose(1, 0, 2)
    qkv_pair = to_peer(qkv_mine, 1)
    head_pair = to_peer(head_table, 1)
    out_rest = along(out_part, 1, 2, 1)
    out_parts = (
        w_out, to_peer(w_out, 1), out_part, out_rest,
        to_peer(out_part, 1), to_peer(out_rest, 1),
    )
    states = [hidden[None]]
    low = 1
    for radix in seq_radices(seq):
        gathered = jnp.concatenate(states, axis=0)
        states = [gathered] + [along(gathered, low, radix, shift) for shift in range(1, radix)]
        low *= radix

    stream_in, att_mine, proj_mine, proj_pair, soft_mine, soft_pair = call(
        functools.partial(attention_kernel, head_dim),
        [((steps, half, width), F32), ((rows, 2 * lanes), BF16)]
        + [((rows, 3 * lanes), BF16)] * 2 + [((pairs * half, lanes), F32)] * 2,
        [
            pltpu.VMEM((steps - 1, half, width), BF16),
            pltpu.VMEM((rows, width), BF16),
            pltpu.VMEM((pairs * half, lanes), BF16),
            pltpu.VMEM((pairs * half, lanes), F32),
        ],
        (partial, partial_side, *looked, qkv_mine, qkv_pair, gain_attn), 4 * rows * qkv_mine.size,
    )
    att_theirs = to_peer(att_mine, 2)
    stream_mid, expo, stats, out_full = call(
        head_kernel,
        [((steps, half, width), F32), ((steps, 2 * half, 2 * vocab_local), BF16), ((half, 128), F32),
         ((tp * lanes, width), BF16)],
        [
            pltpu.VMEM((rows, width), F32),
            pltpu.VMEM((rows, width), BF16),
            pltpu.VMEM((steps, half, 2 * vocab_local), F32),
        ],
        (att_mine, att_theirs, *out_parts, stream_in, gain_head, codes, head_table, head_pair),
        4 * half * head_table.size + 2 * rows * width * width,
    )
    stats_side = to_peer(stats, 2)
    (both,) = call(
        head_back_kernel, [((steps, 2 * half, width), F32)], [],
        (expo, head_table, head_pair), 8 * half * head_table.size,
    )
    att_send, att_keep, mid_sum, losses = call(
        functools.partial(mid_kernel, total),
        [((rows, 2 * lanes), BF16), ((rows, 2 * lanes), F32), ((half, width), F32), ((half, steps), F32)],
        [pltpu.VMEM((rows, width), BF16)],
        (both, stream_mid, gain_head, stats, stats_side, out_full),
        2 * rows * width * width,
    )
    att_recv = to_peer(att_send, 2)
    (part,) = call(
        functools.partial(attention_back_kernel, head_dim),
        [((half, width), BF16)],
        [
            pltpu.VMEM((rows, lanes), BF16),
            pltpu.VMEM((pairs * half, lanes), BF16),
            pltpu.VMEM((pairs * half, lanes), F32),
            pltpu.VMEM((rows, 3 * lanes), BF16),
            pltpu.VMEM((rows, 3 * lanes), BF16),
            pltpu.VMEM((rows, width), F32),
        ],
        (att_keep, att_recv, proj_mine, proj_pair, soft_mine, soft_pair, qkv_mine, qkv_pair,
         stream_in, gain_attn, mid_sum),
        4 * rows * qkv_mine.size,
    )
    size = width // seq
    radices = seq_radices(seq)
    low, rest = 1, seq // radices[0]
    part_side = to_peer(part, 2)
    context_grad, *sends = call(
        functools.partial(sum_kernel, radices[0], 1),
        [((half, width), BF16)] + [((1, rest, half, size), BF16)] * radices[0],
        [pltpu.VMEM((seq, half, size), BF16)],
        (part, part_side), part.size, limit=4,
    )
    for stage, radix in enumerate(radices):
        if stage > 0:
            rest //= radix
            held = sum(item.shape[0] for item in owned)
            sends = call(
                functools.partial(pick_kernel, len(owned), radix, low),
                [((held, rest, half, size), BF16)] * radix, [], owned, part.size, limit=4,
            )
        owned = [sends[0]] + [along(item, low, radix, shift + 1) for shift, item in enumerate(sends[1:])]
        low *= radix
    grad_hidden, row_loss = call(
        hidden_grad_kernel,
        [((frames, w_proj.shape[0]), BF16), ((frames, steps), F32)],
        [pltpu.VMEM((frames, width), BF16)],
        (context_grad, to_peer(context_grad, 1), losses, to_peer(losses, 1), w_proj),
        2 * frames * w_proj.size,
    )
    paired = [to_peer(item, 1) for item in owned]
    held = states[0].shape[0]
    (grad_proj,) = call(
        functools.partial(project_kernel, len(states)),
        [((hidden.shape[1], size), F32)],
        [pltpu.VMEM((len(states), held * frames, size), BF16)],
        (*states, *owned, *paired), 2 * frames * seq * hidden.shape[1] * size, limit=40 if seq > 16 else 12,
    )
    return (row_loss, grad_hidden, grad_proj)


def solution(mesh):
    return jax.shard_map(
        compute,
        mesh=mesh,
        in_specs=(
            P("seq", "tp"),
            P("tp", None),
            P("seq", None),
            P(None, None, "tp"),
            P(None, None, "tp"),
            P("tp", None),
            P(None, None, "tp"),
            P(),
            P(),
        ),
        out_specs=(P("seq", None), P("seq", "tp"), P("tp", "seq")),
        check_vma=False,
    )
```

```python
import functools

import jax
import jax.numpy as jnp
from jax import lax
from jax.experimental import pallas as pl
from jax.experimental.pallas import tpu as pltpu
from jax.sharding import PartitionSpec as P


HEADS = 16
EPS = 1e-06
ROWS = 16
F32 = jnp.float32
BF16 = jnp.bfloat16


def dot(a, b):
    return lax.dot_general(a, b, (((1,), (0,)), ((), ())), preferred_element_type=F32)


def dot_t(a, b):
    return lax.dot_general(a, b, (((1,), (1,)), ((), ())), preferred_element_type=F32)


def inverse_rms(stream):
    return lax.rsqrt(jnp.mean(stream * stream, axis=-1, keepdims=True) + EPS)


def norm_back(stream, gain, cotangent):
    inverse = inverse_rms(stream)
    scaled = gain * cotangent
    along = jnp.mean(stream * scaled, axis=-1, keepdims=True)
    return inverse * scaled - stream * (inverse * inverse * inverse * along)


def head_ones(lanes, head_dim):
    rows = lax.broadcasted_iota(jnp.int32, (lanes, lanes), 0) // head_dim
    columns = lax.broadcasted_iota(jnp.int32, (lanes, lanes), 1) // head_dim
    return jnp.where(rows == columns, 1.0, 0.0).astype(BF16)


def pairs_of(steps):
    return [(a, b) for a in range(steps) for b in range(a + 1)]


def call(kernel, outs, scratch, args, cost, spaces=None, limit=16):
    specs = [pl.BlockSpec(memory_space=pltpu.VMEM) for _ in args]
    for place, space in (spaces or {}).items():
        specs[place] = pl.BlockSpec(memory_space=space)
    return pl.pallas_call(
        kernel,
        out_shape=[jax.ShapeDtypeStruct(shape, dtype) for shape, dtype in outs],
        in_specs=specs,
        out_specs=[pl.BlockSpec(memory_space=pltpu.VMEM) for _ in outs],
        scratch_shapes=scratch,
        cost_estimate=pl.CostEstimate(flops=cost, bytes_accessed=cost // 300, transcendentals=0),
        compiler_params=pltpu.CompilerParams(vmem_limit_bytes=limit * 1024 * 1024),
    )(*args)


def chunk(index):
    return pl.ds(pl.multiple_of(index * ROWS, ROWS), ROWS)


def at_row(base, index):
    return pl.ds(pl.multiple_of(base + index * ROWS, ROWS), ROWS)


def cut_kernel(weight_ref, out_ref, sem):
    rows = out_ref.shape[0]
    place = lax.axis_index("seq") % 2 * rows
    copy = pltpu.make_async_copy(weight_ref.at[pl.ds(pl.multiple_of(place, rows), rows), :], out_ref, sem)
    copy.start()
    copy.wait()


def enter_kernel(
    hidden_ref, weight_ref, codes_ref, table_hbm, mine_ref, other_ref, look_mine, look_other, table_ref, sems,
):
    count, half = look_mine.shape[:2]
    vocab = table_ref.shape[1]
    core = lax.axis_index("tp") % 2
    copies = [pltpu.make_async_copy(table_hbm.at[k], table_ref.at[k], sems.at[k]) for k in range(count)]
    for copy in copies:
        copy.start()
    low = pl.ds(pl.multiple_of(core * half, half), half)
    high = pl.ds(pl.multiple_of((1 - core) * half, half), half)
    partial = dot(jnp.concatenate([hidden_ref[low, :], hidden_ref[high, :]], axis=0), weight_ref[...])
    mine_ref[...] = partial[:half]
    other_ref[...] = partial[half:].astype(BF16)
    codes = jnp.concatenate([codes_ref[low, :], codes_ref[high, :]], axis=0)
    lanes = lax.broadcasted_iota(jnp.int32, (2 * half, vocab), 1)
    for k in range(count):
        chosen = jnp.where(lanes == codes[:, k : k + 1], 1.0, 0.0).astype(BF16)
        copies[k].wait()
        found = dot(chosen, table_ref[k]).astype(BF16)
        look_mine[k] = found[:half]
        look_other[k] = found[half:]


def join_kernel(mine_ref, other_ref, out_ref):
    out_ref[...] = (mine_ref[...] + other_ref[...].astype(F32)).astype(BF16)


def attention_kernel(
    head_dim, own_ref, side_ref, look0, look1, look2, look3, qkv_mine, qkv_pair, gain_ref,
    stream_ref, att_ref, proj_mine, proj_pair, soft_mine, soft_pair,
    look_ref, normed_ref, product_ref, score_ref,
):
    steps, half, _ = stream_ref.shape
    rank = lax.axis_index("tp")
    lanes = look0.shape[2]
    chunks = half // ROWS
    pairs = pairs_of(steps)
    scale = head_dim ** (-0.5)
    for j, look in enumerate((look0, look1, look2, look3)):
        place = pl.ds(pl.multiple_of((rank ^ j) * lanes, lanes), lanes)
        for k in range(steps - 1):
            look_ref[k, :, place] = look[k]

    def enter(i, carry):
        context = own_ref[chunk(i), :].astype(F32) + side_ref[chunk(i), :].astype(F32)
        for k in range(steps):
            stream = context if k == 0 else context + look_ref[k - 1, chunk(i), :].astype(F32)
            stream_ref[k, chunk(i), :] = stream
            normed = stream * inverse_rms(stream) * gain_ref[...]
            normed_ref[at_row(k * half, i), :] = normed.astype(BF16)
        return carry

    lax.fori_loop(0, chunks, enter, 0)
    ones = head_ones(lanes, head_dim)
    for j, (weight, proj, soft) in enumerate(
        ((qkv_mine, proj_mine, soft_mine), (qkv_pair, proj_pair, soft_pair))
    ):
        for part in range(3):
            proj[:, part * lanes : (part + 1) * lanes] = dot(normed_ref[...], weight[part]).astype(BF16)

        def multiply(i, carry):
            rows = [at_row(k * half, i) for k in range(steps)]
            query = [proj[row, 0:lanes] for row in rows]
            keys = [proj[row, lanes : 2 * lanes] for row in rows]
            for p, (a, b) in enumerate(pairs):
                product_ref[at_row(p * half, i), :] = query[a] * keys[b]
            return carry

        lax.fori_loop(0, chunks, multiply, 0)
        score_ref[...] = dot(product_ref[...], ones) * scale

        def weigh(i, carry):
            rows = [at_row(k * half, i) for k in range(steps)]
            values = [proj[row, 2 * lanes : 3 * lanes].astype(F32) for row in rows]
            for a in range(steps):
                first = pairs.index((a, 0))
                row = [score_ref[at_row((first + b) * half, i), :] for b in range(a + 1)]
                top = functools.reduce(jnp.maximum, row)
                row = [jnp.exp(item - top) for item in row]
                total = functools.reduce(jnp.add, row)
                mixed = 0.0
                for b in range(a + 1):
                    weight_ab = row[b] / total
                    soft[at_row((first + b) * half, i), :] = weight_ab
                    mixed = mixed + weight_ab.astype(BF16).astype(F32) * values[b]
                att_ref[rows[a], j * lanes : (j + 1) * lanes] = mixed.astype(BF16)
            return carry

        lax.fori_loop(0, chunks, weigh, 0)


def mix_kernel(
    att_ref, own_ref, pair_ref, part_a, part_b, part_c, part_d, stream_ref, full_ref, mixed_ref, sum_ref,
):
    steps, half, _ = stream_ref.shape
    lanes, cut = own_ref.shape[0], part_a.shape[0]
    place = lax.axis_index("seq") % 2
    full_ref[0:lanes, :] = own_ref[...]
    full_ref[lanes : 2 * lanes, :] = pair_ref[...]
    for base, first, second in ((2 * lanes, part_a, part_b), (3 * lanes, part_c, part_d)):
        full_ref[pl.ds(pl.multiple_of(base + place * cut, cut), cut), :] = first[...]
        full_ref[pl.ds(pl.multiple_of(base + (1 - place) * cut, cut), cut), :] = second[...]
    sum_ref[...] = dot(att_ref[...], full_ref[0 : 2 * lanes, :])
    for k in range(steps):
        mixed_ref[k] = stream_ref[k] + sum_ref[k * half : (k + 1) * half, :]


def head_kernel(
    att_theirs, full_ref, stream_ref, gain_ref, codes_ref, head_mine, head_pair,
    mid_ref, expo_ref, stats_ref, mixed_ref, normed_ref, logit_ref,
):
    steps, half, _ = stream_ref.shape
    rank = lax.axis_index("tp")
    core = rank % 2
    vocab = head_mine.shape[2]
    chunks = half // ROWS
    middle = full_ref.shape[0] // 2
    mixed_ref[...] = dot(att_theirs[...], full_ref[middle : 2 * middle, :])

    def enter(i, carry):
        for k in range(steps):
            stream = stream_ref[k, chunk(i), :] + mixed_ref[at_row(k * half, i), :]
            mid_ref[k, chunk(i), :] = stream
            normed = stream * inverse_rms(stream) * gain_ref[...]
            normed_ref[at_row(k * half, i), :] = normed.astype(BF16)
        return carry

    lax.fori_loop(0, chunks, enter, 0)
    for k in range(steps):
        normed = normed_ref[k * half : (k + 1) * half, :]
        logit_ref[k, :, 0:vocab] = dot(normed, head_mine[k])
        logit_ref[k, :, vocab : 2 * vocab] = dot(normed, head_pair[k])

    def leave(i, carry):
        lanes = lax.broadcasted_iota(jnp.int32, (ROWS, 2 * vocab), 1)
        ids = jnp.where(lanes < vocab, lanes + rank * vocab, lanes - vocab + (rank ^ 1) * vocab)
        spots = lax.broadcasted_iota(jnp.int32, (ROWS, stats_ref.shape[1]), 1)
        stats = jnp.zeros((ROWS, stats_ref.shape[1]), F32)
        codes = codes_ref[pl.ds(pl.multiple_of(core * half + i * ROWS, ROWS), ROWS), :]
        for k in range(steps):
            logits = logit_ref[k, chunk(i), :]
            hits = ids == codes[:, k : k + 1]
            top = jnp.max(logits, axis=-1, keepdims=True)
            expo = jnp.exp(logits - top)
            total = jnp.sum(expo, axis=-1, keepdims=True)
            target = jnp.sum(jnp.where(hits, logits, 0.0), axis=-1, keepdims=True)
            expo_ref[k, chunk(i), :] = jnp.where(hits, 0.0, expo).astype(BF16)
            expo_ref[k, at_row(half, i), :] = jnp.where(hits, 1.0, 0.0).astype(BF16)
            for j, value in enumerate((top, total, target)):
                stats = jnp.where(spots == 3 * k + j, value, stats)
        stats_ref[chunk(i), :] = stats
        return carry

    lax.fori_loop(0, chunks, leave, 0)


def head_back_kernel(expo_ref, head_mine, head_pair, both_ref):
    vocab = head_mine.shape[2]
    for k in range(both_ref.shape[0]):
        both_ref[k] = dot_t(expo_ref[k, :, 0:vocab], head_mine[k]) + dot_t(
            expo_ref[k, :, vocab : 2 * vocab], head_pair[k]
        )


def mid_kernel(
    frames_total, both_ref, mid_ref, gain_ref, stats_ref, stats_side, out_ref,
    send_ref, low_ref, sum_ref, loss_ref,
):
    steps, half, _ = mid_ref.shape

    def leave(i, carry):
        mine = stats_ref[chunk(i), :]
        theirs = stats_side[chunk(i), :]
        spots = lax.broadcasted_iota(jnp.int32, (ROWS, steps), 1)
        losses = jnp.zeros((ROWS, steps), F32)
        added = 0.0
        for k in range(steps):
            top_a, sum_a, target_a = [mine[:, 3 * k + j : 3 * k + j + 1] for j in range(3)]
            top_b, sum_b, target_b = [theirs[:, 3 * k + j : 3 * k + j + 1] for j in range(3)]
            top = jnp.maximum(top_a, top_b)
            log_total = top + jnp.log(sum_a * jnp.exp(top_a - top) + sum_b * jnp.exp(top_b - top))
            target = target_a + target_b
            losses = jnp.where(spots == k, log_total - target, losses)
            part = both_ref[k, chunk(i), :] * (jnp.exp(top_a - log_total) / frames_total)
            hit = (jnp.exp(target - log_total) - 1.0) / frames_total
            part = part + both_ref[k, at_row(half, i), :] * hit
            grad = norm_back(mid_ref[k, chunk(i), :], gain_ref[...], part)
            low_ref[at_row(k * half, i), :] = grad.astype(BF16)
            added = added + grad
        sum_ref[chunk(i), :] = added
        loss_ref[chunk(i), :] = losses
        return carry

    lax.fori_loop(0, half // ROWS, leave, 0)
    middle = out_ref.shape[0] // 2
    send_ref[...] = dot_t(low_ref[...], out_ref[middle : 2 * middle, :]).astype(BF16)


def keep_kernel(low_ref, out_ref, loss_mine, loss_pair, keep_ref, loss_ref):
    half = loss_mine.shape[0]
    core = lax.axis_index("tp") % 2
    loss_ref[pl.ds(pl.multiple_of(core * half, half), half), :] = loss_mine[...]
    loss_ref[pl.ds(pl.multiple_of((1 - core) * half, half), half), :] = loss_pair[...]
    keep_ref[...] = dot_t(low_ref[...], out_ref[0 : out_ref.shape[0] // 2, :])


def attention_back_kernel(
    head_dim, keep_ref, recv_ref, proj_mine, proj_pair, soft_mine, soft_pair, qkv_mine, qkv_pair,
    stream_ref, gain_ref, sum_ref, part_ref, *refs,
):
    blocks_ref, grad_ref, product_ref, prob_ref, back_mine, back_pair, normin_ref = refs[-7:]
    sends = refs[:-7]
    radix = len(sends) + 1
    digit = lax.axis_index("seq") % radix
    steps, half, _ = stream_ref.shape
    lanes = keep_ref.shape[1] // 2
    chunks = half // ROWS
    pairs = pairs_of(steps)
    scale = head_dim ** (-0.5)
    ones = head_ones(lanes, head_dim)
    for j, (proj, soft, back) in enumerate(
        ((proj_mine, soft_mine, back_mine), (proj_pair, soft_pair, back_pair))
    ):
        span = slice(j * lanes, (j + 1) * lanes)

        def multiply(i, carry):
            rows = [at_row(k * half, i) for k in range(steps)]
            values = [proj[row, 2 * lanes : 3 * lanes] for row in rows]
            for a in range(steps):
                grad = (keep_ref[rows[a], span] + recv_ref[rows[a], span].astype(F32)).astype(BF16)
                grad_ref[rows[a], :] = grad
                for b in range(a + 1):
                    product_ref[at_row(pairs.index((a, b)) * half, i), :] = grad * values[b]
            return carry

        lax.fori_loop(0, chunks, multiply, 0)
        prob_ref[...] = dot(product_ref[...], ones)

        def spread(i, carry):
            rows = [at_row(k * half, i) for k in range(steps)]
            query_grad = [0.0] * steps
            key_grad = [0.0] * steps
            value_grad = [0.0] * steps
            for a in range(steps):
                first = pairs.index((a, 0))
                weights = [soft[at_row((first + b) * half, i), :] for b in range(a + 1)]
                probs = [prob_ref[at_row((first + b) * half, i), :] for b in range(a + 1)]
                inner = functools.reduce(jnp.add, [w * p for w, p in zip(weights, probs)])
                grad = grad_ref[rows[a], :].astype(F32)
                query = proj[rows[a], 0:lanes].astype(F32)
                for b in range(a + 1):
                    score = (weights[b] * (probs[b] - inner) * scale).astype(BF16).astype(F32)
                    key = proj[rows[b], lanes : 2 * lanes].astype(F32)
                    query_grad[a] = query_grad[a] + score * key
                    key_grad[b] = key_grad[b] + score * query
                    value_grad[b] = value_grad[b] + weights[b].astype(BF16).astype(F32) * grad
            for k in range(steps):
                back[rows[k], 0:lanes] = query_grad[k].astype(BF16)
                back[rows[k], lanes : 2 * lanes] = key_grad[k].astype(BF16)
                back[rows[k], 2 * lanes : 3 * lanes] = value_grad[k].astype(BF16)
            return carry

        lax.fori_loop(0, chunks, spread, 0)
    total = 0.0
    for back, weight in ((back_mine, qkv_mine), (back_pair, qkv_pair)):
        for part in range(3):
            total = total + dot_t(back[:, part * lanes : (part + 1) * lanes], weight[part])
    normin_ref[...] = total

    def leave(i, carry):
        part = sum_ref[chunk(i), :]
        for k in range(steps):
            part = part + norm_back(stream_ref[k, chunk(i), :], gain_ref[...], normin_ref[at_row(k * half, i), :])
        part = part.astype(BF16)
        part_ref[chunk(i), :] = part
        count, _, size = blocks_ref.shape
        for j in range(count):
            blocks_ref[j, chunk(i), :] = part[:, j * size : (j + 1) * size]
        return carry

    lax.fori_loop(0, chunks, leave, 0)
    for shift, out in enumerate(sends):
        for w in range(out.shape[0]):
            out[w] = blocks_ref[w * radix + (digit + shift + 1) % radix]


def sum_kernel(first, radix, *refs):
    part_ref, side_ref = refs[:2]
    near, far = refs[2 : first + 1], refs[first + 1 : 2 * first]
    grad_ref, *outs = refs[2 * first : 2 * first + 1 + radix]
    blocks_ref, held_ref = refs[2 * first + 1 + radix :]
    count, _, size = blocks_ref.shape
    rest = count // first
    digit = lax.axis_index("seq") % first
    upper = lax.axis_index("seq") // first % radix
    grad = (part_ref[...].astype(F32) + side_ref[...].astype(F32)).astype(BF16)
    grad_ref[...] = grad
    for j in range(count):
        blocks_ref[j] = grad[:, j * size : (j + 1) * size]
    for w in range(rest):
        held_ref[0, w] = blocks_ref[w * first + digit]
    for place, (one, two) in enumerate(zip(near, far)):
        held_ref[place + 1] = (one[...].astype(F32) + two[...].astype(F32)).astype(BF16)
    for shift, out in enumerate(outs):
        for i in range(first):
            for w in range(rest // radix):
                out[i, w] = held_ref[i, w * radix + (upper + shift) % radix]


def pick_kernel(count, radix, low, *refs):
    digit = lax.axis_index("seq") // low % radix
    for shift, out in enumerate(refs[count:]):
        place = 0
        for item in refs[:count]:
            for q in range(item.shape[0]):
                for w in range(item.shape[1] // radix):
                    out[place, w] = item[q, w * radix + (digit + shift) % radix]
                place += 1


def hidden_grad_kernel(mine_ref, pair_ref, weight_ref, out_ref, full_ref):
    half = mine_ref.shape[0]
    core = lax.axis_index("tp") % 2
    full_ref[pl.ds(pl.multiple_of(core * half, half), half), :] = mine_ref[...]
    full_ref[pl.ds(pl.multiple_of((1 - core) * half, half), half), :] = pair_ref[...]
    out_ref[...] = dot_t(full_ref[...], weight_ref[...]).astype(BF16)


def project_kernel(radices, *refs):
    count = radices[-1]
    out_ref, grads_ref = refs[-2:]
    mine, pair = refs[-2 - 2 * count : -2 - count], refs[-2 - count : -2]
    states = refs[: -2 - 2 * count]
    half = mine[0].shape[2]
    core = lax.axis_index("tp") % 2
    index = lax.axis_index("seq")
    held = mine[0].shape[0]
    for p, (low, high) in enumerate(zip(mine, pair)):
        for q in range(held):
            grads_ref[p * held + q, pl.ds(pl.multiple_of(core * half, half), half), :] = low[q, 0]
            grads_ref[p * held + q, pl.ds(pl.multiple_of((1 - core) * half, half), half), :] = high[q, 0]
    total = 0.0
    for p in range(count * held):
        if len(states) > 1:
            rows = states[p][0]
        else:
            source, left, low = 0, p, 1
            for radix in radices:
                source = source + (index // low + radix - left % radix) % radix * low
                left //= radix
                low *= radix
            rows = states[0][source]
        total = total + lax.dot_general(
            grads_ref[p], rows, (((0,), (0,)), ((), ())), preferred_element_type=F32
        )
    out_ref[...] = total.T


def seq_radices(size):
    radices = []
    while size % 4 == 0:
        radices.append(4)
        size //= 4
    return [size] + radices if size > 1 else radices


def compute(hidden, w_proj, codes, embed_table, w_qkv, w_out, head_table, gain_attn, gain_head):
    frames, steps = codes.shape
    half = frames // 2
    width = w_proj.shape[1]
    head_dim = width // HEADS
    vocab_local = head_table.shape[2]
    lanes = w_qkv.shape[2]
    tp = lax.axis_size("tp")
    seq = lax.axis_size("seq")
    total = float(frames * seq * steps)
    pairs = len(pairs_of(steps))
    rows = steps * half
    gain_attn = gain_attn.reshape(1, width)
    gain_head = gain_head.reshape(1, width)

    def to_peer(value, flip):
        return lax.ppermute(value, "tp", [(i, i ^ flip) for i in range(tp)])

    def along(value, low, radix, shift, flip=0):
        route = []
        for i in range(seq):
            digit = i // low % radix
            there = i + ((digit + shift) % radix - digit) * low
            route += [(i * tp + j, there * tp + (j ^ flip)) for j in range(tp)]
        return lax.ppermute(value, ("seq", "tp"), route)

    cut = lanes // 2
    (out_part,) = call(
        cut_kernel, [((cut, width), BF16)], [pltpu.SemaphoreType.DMA], (w_out,), 6 * 10**9, {0: pltpu.HBM}, limit=4
    )
    out_part = to_peer(out_part, 2)
    partial, partial_other, looked, looked_other = call(
        enter_kernel,
        [((half, width), F32), ((half, width), BF16)] + [((steps - 1, half, lanes), BF16)] * 2,
        [pltpu.VMEM(embed_table.shape, BF16), pltpu.SemaphoreType.DMA((steps - 1,))],
        (hidden, w_proj, codes, embed_table), 6 * 10**9, {3: pltpu.HBM}, limit=60,
    )
    (partial,) = call(
        join_kernel, [((half, width), BF16)], [],
        (partial, to_peer(partial_other, 1)), partial.size, limit=4,
    )
    partial_side = to_peer(partial, 2)
    looked = [looked, to_peer(looked_other, 1), to_peer(looked, 2), to_peer(looked_other, 3)]

    qkv_mine = w_qkv.transpose(1, 0, 2)
    qkv_pair = to_peer(qkv_mine, 1)
    head_pair = to_peer(head_table, 1)
    out_rest = along(out_part, 1, 2, 1)
    out_parts = (
        w_out, to_peer(w_out, 1), out_part, out_rest,
        to_peer(out_part, 1), to_peer(out_rest, 1),
    )
    radices = seq_radices(seq)
    if seq > 16:
        states = [lax.all_gather(hidden, "seq")]
    else:
        states, low = [hidden[None]], seq
        for radix in reversed(radices):
            low //= radix
            states = [
                item if shift == 0 else along(item, low, radix, shift)
                for item in states
                for shift in range(radix)
            ]

    stream_in, att_mine, proj_mine, proj_pair, soft_mine, soft_pair = call(
        functools.partial(attention_kernel, head_dim),
        [((steps, half, width), F32), ((rows, 2 * lanes), BF16)]
        + [((rows, 3 * lanes), BF16)] * 2 + [((pairs * half, lanes), F32)] * 2,
        [
            pltpu.VMEM((steps - 1, half, width), BF16),
            pltpu.VMEM((rows, width), BF16),
            pltpu.VMEM((pairs * half, lanes), BF16),
            pltpu.VMEM((pairs * half, lanes), F32),
        ],
        (partial, partial_side, *looked, qkv_mine, qkv_pair, gain_attn), 4 * rows * qkv_mine.size,
    )
    att_theirs = to_peer(att_mine, 2)
    out_full, mixed = call(
        mix_kernel, [((tp * lanes, width), BF16), ((steps, half, width), F32)],
        [pltpu.VMEM((rows, width), F32)],
        (att_mine, *out_parts, stream_in), rows * width * width,
    )
    stream_mid, expo, stats = call(
        head_kernel,
        [((steps, half, width), F32), ((steps, 2 * half, 2 * vocab_local), BF16), ((half, 128), F32)],
        [
            pltpu.VMEM((rows, width), F32),
            pltpu.VMEM((rows, width), BF16),
            pltpu.VMEM((steps, half, 2 * vocab_local), F32),
        ],
        (att_theirs, out_full, mixed, gain_head, codes, head_table, head_pair),
        4 * half * head_table.size + rows * width * width,
    )
    stats_side = to_peer(stats, 2)
    (both,) = call(
        head_back_kernel, [((steps, 2 * half, width), F32)], [],
        (expo, head_table, head_pair), 8 * half * head_table.size,
    )
    att_send, mid_low, mid_sum, losses = call(
        functools.partial(mid_kernel, total),
        [((rows, 2 * lanes), BF16), ((rows, width), BF16), ((half, width), F32), ((half, steps), F32)],
        [], (both, stream_mid, gain_head, stats, stats_side, out_full), rows * width * width,
    )
    att_recv = to_peer(att_send, 2)
    att_keep, row_loss = call(
        keep_kernel, [((rows, 2 * lanes), F32), ((frames, steps), F32)], [],
        (mid_low, out_full, losses, to_peer(losses, 1)), rows * width * width,
    )
    size = width // seq
    first, rest = radices[0], seq // radices[0]
    part, *sends = call(
        functools.partial(attention_back_kernel, head_dim),
        [((half, width), BF16)] + [((rest, half, size), BF16)] * (first - 1),
        [
            pltpu.VMEM((seq, half, size), BF16),
            pltpu.VMEM((rows, lanes), BF16),
            pltpu.VMEM((pairs * half, lanes), BF16),
            pltpu.VMEM((pairs * half, lanes), F32),
            pltpu.VMEM((rows, 3 * lanes), BF16),
            pltpu.VMEM((rows, 3 * lanes), BF16),
            pltpu.VMEM((rows, width), F32),
        ],
        (att_keep, att_recv, proj_mine, proj_pair, soft_mine, soft_pair, qkv_mine, qkv_pair,
         stream_in, gain_attn, mid_sum),
        4 * rows * qkv_mine.size,
    )
    part_side = to_peer(part, 2)
    near = [along(item, 1, first, shift + 1) for shift, item in enumerate(sends)]
    far = [along(item, 1, first, shift + 1, 2) for shift, item in enumerate(sends)]
    part_side, *states = lax.optimization_barrier((part_side, *states))
    context_grad, *sends = call(
        functools.partial(sum_kernel, first, radices[1]),
        [((half, width), BF16)] + [((first, rest // radices[1], half, size), BF16)] * radices[1],
        [pltpu.VMEM((seq, half, size), BF16), pltpu.VMEM((first, rest, half, size), BF16)],
        (part, part_side, *near, *far), part.size, limit=4,
    )
    low = first
    for stage, radix in enumerate(radices):
        if stage == 0:
            continue
        rest //= radix
        if stage > 1:
            held = sum(item.shape[0] for item in owned)
            sends = call(
                functools.partial(pick_kernel, len(owned), radix, low),
                [((held, rest, half, size), BF16)] * radix, [], owned, part.size, limit=4,
            )
        owned = [sends[0]] + [along(item, low, radix, shift + 1) for shift, item in enumerate(sends[1:])]
        low *= radix
    (grad_hidden,) = call(
        hidden_grad_kernel, [((frames, w_proj.shape[0]), BF16)],
        [pltpu.VMEM((frames, width), BF16)],
        (context_grad, to_peer(context_grad, 1), w_proj), 2 * frames * w_proj.size,
    )
    paired = [to_peer(item, 1) for item in owned]
    (grad_proj,) = call(
        functools.partial(project_kernel, tuple(radices)),
        [((hidden.shape[1], size), F32)],
        [pltpu.VMEM((seq, frames, size), BF16)],
        (*states, *owned, *paired), 2 * frames * seq * hidden.shape[1] * size, limit=40 if seq > 16 else 12,
    )
    return (row_loss, grad_hidden, grad_proj)


def solution(mesh):
    return jax.shard_map(
        compute,
        mesh=mesh,
        in_specs=(
            P("seq", "tp"),
            P("tp", None),
            P("seq", None),
            P(None, None, "tp"),
            P(None, None, "tp"),
            P("tp", None),
            P(None, None, "tp"),
            P(),
            P(),
        ),
        out_specs=(P("seq", None), P("seq", "tp"), P("tp", "seq")),
        check_vma=False,
    )
```

```python
import functools

import jax
import jax.numpy as jnp
from jax import lax
from jax.experimental import pallas as pl
from jax.experimental.pallas import tpu as pltpu
from jax.sharding import PartitionSpec as P


HEADS = 16
EPS = 1e-06
ROWS = 16
F32 = jnp.float32
BF16 = jnp.bfloat16


def dot(a, b):
    return lax.dot_general(a, b, (((1,), (0,)), ((), ())), preferred_element_type=F32)


def dot_t(a, b):
    return lax.dot_general(a, b, (((1,), (1,)), ((), ())), preferred_element_type=F32)


def inverse_rms(stream):
    return lax.rsqrt(jnp.mean(stream * stream, axis=-1, keepdims=True) + EPS)


def norm_back(stream, gain, cotangent):
    inverse = inverse_rms(stream)
    scaled = gain * cotangent
    along = jnp.mean(stream * scaled, axis=-1, keepdims=True)
    return inverse * scaled - stream * (inverse * inverse * inverse * along)


def head_ones(lanes, head_dim):
    rows = lax.broadcasted_iota(jnp.int32, (lanes, lanes), 0) // head_dim
    columns = lax.broadcasted_iota(jnp.int32, (lanes, lanes), 1) // head_dim
    return jnp.where(rows == columns, 1.0, 0.0).astype(BF16)


def pairs_of(steps):
    return [(a, b) for a in range(steps) for b in range(a + 1)]


def call(kernel, outs, scratch, args, cost, spaces=None, limit=16):
    specs = [pl.BlockSpec(memory_space=pltpu.VMEM) for _ in args]
    for place, space in (spaces or {}).items():
        specs[place] = pl.BlockSpec(memory_space=space)
    return pl.pallas_call(
        kernel,
        out_shape=[jax.ShapeDtypeStruct(shape, dtype) for shape, dtype in outs],
        in_specs=specs,
        out_specs=[pl.BlockSpec(memory_space=pltpu.VMEM) for _ in outs],
        scratch_shapes=scratch,
        cost_estimate=pl.CostEstimate(flops=cost, bytes_accessed=cost // 300, transcendentals=0),
        compiler_params=pltpu.CompilerParams(vmem_limit_bytes=limit * 1024 * 1024),
    )(*args)


def chunk(index):
    return pl.ds(pl.multiple_of(index * ROWS, ROWS), ROWS)


def at_row(base, index):
    return pl.ds(pl.multiple_of(base + index * ROWS, ROWS), ROWS)


def cut_kernel(weight_ref, out_ref, sem):
    rows = out_ref.shape[0]
    place = lax.axis_index("seq") % 2 * rows
    copy = pltpu.make_async_copy(weight_ref.at[pl.ds(pl.multiple_of(place, rows), rows), :], out_ref, sem)
    copy.start()
    copy.wait()


def context_kernel(hidden_ref, weight_ref, mine_ref, other_ref):
    half = mine_ref.shape[0]
    core = lax.axis_index("tp") % 2
    low = hidden_ref[pl.ds(pl.multiple_of(core * half, half), half), :]
    high = hidden_ref[pl.ds(pl.multiple_of((1 - core) * half, half), half), :]
    partial = dot(jnp.concatenate([low, high], axis=0), weight_ref[...])
    mine_ref[...] = partial[:half]
    other_ref[...] = partial[half:].astype(BF16)


def lookup_kernel(codes_ref, table_ref, mine_ref, other_ref, code_ref):
    count, half = mine_ref.shape[:2]
    vocab = table_ref.shape[1]
    core = lax.axis_index("tp") % 2
    code_ref[...] = codes_ref[...].T
    low = code_ref[pl.ds(pl.multiple_of(core * half, half), half), :]
    high = code_ref[pl.ds(pl.multiple_of((1 - core) * half, half), half), :]
    codes = jnp.concatenate([low, high], axis=0)
    lanes = lax.broadcasted_iota(jnp.int32, (2 * half, vocab), 1)
    for k in range(count):
        chosen = jnp.where(lanes == codes[:, k : k + 1], 1.0, 0.0).astype(BF16)
        found = dot(chosen, table_ref[k]).astype(BF16)
        mine_ref[k] = found[:half]
        other_ref[k] = found[half:]


def join_kernel(mine_ref, other_ref, out_ref):
    out_ref[...] = (mine_ref[...] + other_ref[...].astype(F32)).astype(BF16)


def attention_kernel(
    head_dim, own_ref, side_ref, look0, look1, look2, look3, qkv_mine, qkv_pair, gain_ref,
    stream_ref, att_ref, proj_mine, proj_pair, soft_mine, soft_pair,
    look_ref, normed_ref, product_ref, score_ref,
):
    steps, half, _ = stream_ref.shape
    rank = lax.axis_index("tp")
    lanes = look0.shape[2]
    chunks = half // ROWS
    pairs = pairs_of(steps)
    scale = head_dim ** (-0.5)
    for j, look in enumerate((look0, look1, look2, look3)):
        place = pl.ds(pl.multiple_of((rank ^ j) * lanes, lanes), lanes)
        for k in range(steps - 1):
            look_ref[k, :, place] = look[k]

    def enter(i, carry):
        context = own_ref[chunk(i), :].astype(F32) + side_ref[chunk(i), :].astype(F32)
        for k in range(steps):
            stream = context if k == 0 else context + look_ref[k - 1, chunk(i), :].astype(F32)
            stream_ref[k, chunk(i), :] = stream
            normed = stream * inverse_rms(stream) * gain_ref[...]
            normed_ref[at_row(k * half, i), :] = normed.astype(BF16)
        return carry

    lax.fori_loop(0, chunks, enter, 0)
    ones = head_ones(lanes, head_dim)
    for j, (weight, proj, soft) in enumerate(
        ((qkv_mine, proj_mine, soft_mine), (qkv_pair, proj_pair, soft_pair))
    ):
        for part in range(3):
            proj[:, part * lanes : (part + 1) * lanes] = dot(normed_ref[...], weight[part]).astype(BF16)

        def multiply(i, carry):
            rows = [at_row(k * half, i) for k in range(steps)]
            query = [proj[row, 0:lanes] for row in rows]
            keys = [proj[row, lanes : 2 * lanes] for row in rows]
            for p, (a, b) in enumerate(pairs):
                product_ref[at_row(p * half, i), :] = query[a] * keys[b]
            return carry

        lax.fori_loop(0, chunks, multiply, 0)
        score_ref[...] = dot(product_ref[...], ones) * scale

        def weigh(i, carry):
            rows = [at_row(k * half, i) for k in range(steps)]
            values = [proj[row, 2 * lanes : 3 * lanes].astype(F32) for row in rows]
            for a in range(steps):
                first = pairs.index((a, 0))
                row = [score_ref[at_row((first + b) * half, i), :] for b in range(a + 1)]
                top = functools.reduce(jnp.maximum, row)
                row = [jnp.exp(item - top) for item in row]
                total = functools.reduce(jnp.add, row)
                mixed = 0.0
                for b in range(a + 1):
                    weight_ab = row[b] / total
                    soft[at_row((first + b) * half, i), :] = weight_ab
                    mixed = mixed + weight_ab.astype(BF16).astype(F32) * values[b]
                att_ref[rows[a], j * lanes : (j + 1) * lanes] = mixed.astype(BF16)
            return carry

        lax.fori_loop(0, chunks, weigh, 0)


def mix_kernel(
    att_ref, own_ref, pair_ref, part_a, part_b, part_c, part_d, stream_ref, full_ref, mixed_ref, sum_ref,
):
    steps, half, _ = stream_ref.shape
    lanes, cut = own_ref.shape[0], part_a.shape[0]
    place = lax.axis_index("seq") % 2
    full_ref[0:lanes, :] = own_ref[...]
    full_ref[lanes : 2 * lanes, :] = pair_ref[...]
    for base, first, second in ((2 * lanes, part_a, part_b), (3 * lanes, part_c, part_d)):
        full_ref[pl.ds(pl.multiple_of(base + place * cut, cut), cut), :] = first[...]
        full_ref[pl.ds(pl.multiple_of(base + (1 - place) * cut, cut), cut), :] = second[...]
    sum_ref[...] = dot(att_ref[...], full_ref[0 : 2 * lanes, :])
    for k in range(steps):
        mixed_ref[k] = stream_ref[k] + sum_ref[k * half : (k + 1) * half, :]


def head_kernel(
    att_theirs, full_ref, stream_ref, gain_ref, codes_ref, head_mine, head_pair,
    mid_ref, expo_ref, stats_ref, mixed_ref, normed_ref, logit_ref, code_ref,
):
    steps, half, _ = stream_ref.shape
    code_ref[...] = codes_ref[...].T
    rank = lax.axis_index("tp")
    core = rank % 2
    vocab = head_mine.shape[2]
    chunks = half // ROWS
    middle = full_ref.shape[0] // 2
    mixed_ref[...] = dot(att_theirs[...], full_ref[middle : 2 * middle, :])

    def enter(i, carry):
        for k in range(steps):
            stream = stream_ref[k, chunk(i), :] + mixed_ref[at_row(k * half, i), :]
            mid_ref[k, chunk(i), :] = stream
            normed = stream * inverse_rms(stream) * gain_ref[...]
            normed_ref[at_row(k * half, i), :] = normed.astype(BF16)
        return carry

    lax.fori_loop(0, chunks, enter, 0)
    for k in range(steps):
        normed = normed_ref[k * half : (k + 1) * half, :]
        logit_ref[k, :, 0:vocab] = dot(normed, head_mine[k])
        logit_ref[k, :, vocab : 2 * vocab] = dot(normed, head_pair[k])

    def leave(i, carry):
        lanes = lax.broadcasted_iota(jnp.int32, (ROWS, 2 * vocab), 1)
        ids = jnp.where(lanes < vocab, lanes + rank * vocab, lanes - vocab + (rank ^ 1) * vocab)
        spots = lax.broadcasted_iota(jnp.int32, (ROWS, stats_ref.shape[1]), 1)
        stats = jnp.zeros((ROWS, stats_ref.shape[1]), F32)
        codes = code_ref[pl.ds(pl.multiple_of(core * half + i * ROWS, ROWS), ROWS), :]
        for k in range(steps):
            logits = logit_ref[k, chunk(i), :]
            hits = ids == codes[:, k : k + 1]
            top = jnp.max(logits, axis=-1, keepdims=True)
            expo = jnp.exp(logits - top)
            total = jnp.sum(expo, axis=-1, keepdims=True)
            target = jnp.sum(jnp.where(hits, logits, 0.0), axis=-1, keepdims=True)
            expo_ref[k, chunk(i), :] = jnp.where(hits, 0.0, expo).astype(BF16)
            expo_ref[k, at_row(half, i), :] = jnp.where(hits, 1.0, 0.0).astype(BF16)
            for j, value in enumerate((top, total, target)):
                stats = jnp.where(spots == 3 * k + j, value, stats)
        stats_ref[chunk(i), :] = stats
        return carry

    lax.fori_loop(0, chunks, leave, 0)


def head_back_kernel(expo_ref, head_mine, head_pair, both_ref):
    vocab = head_mine.shape[2]
    for k in range(both_ref.shape[0]):
        both_ref[k] = dot_t(expo_ref[k, :, 0:vocab], head_mine[k]) + dot_t(
            expo_ref[k, :, vocab : 2 * vocab], head_pair[k]
        )


def mid_kernel(
    frames_total, both_ref, mid_ref, gain_ref, stats_ref, stats_side, out_ref,
    send_ref, low_ref, sum_ref, loss_ref,
):
    steps, half, _ = mid_ref.shape

    def leave(i, carry):
        mine = stats_ref[chunk(i), :]
        theirs = stats_side[chunk(i), :]
        spots = lax.broadcasted_iota(jnp.int32, loss_ref[chunk(i), :].shape, 1)
        losses = jnp.zeros(spots.shape, F32)
        added = 0.0
        for k in range(steps):
            top_a, sum_a, target_a = [mine[:, 3 * k + j : 3 * k + j + 1] for j in range(3)]
            top_b, sum_b, target_b = [theirs[:, 3 * k + j : 3 * k + j + 1] for j in range(3)]
            top = jnp.maximum(top_a, top_b)
            log_total = top + jnp.log(sum_a * jnp.exp(top_a - top) + sum_b * jnp.exp(top_b - top))
            target = target_a + target_b
            losses = jnp.where(spots == k, log_total - target, losses)
            part = both_ref[k, chunk(i), :] * (jnp.exp(top_a - log_total) / frames_total)
            hit = (jnp.exp(target - log_total) - 1.0) / frames_total
            part = part + both_ref[k, at_row(half, i), :] * hit
            grad = norm_back(mid_ref[k, chunk(i), :], gain_ref[...], part)
            low_ref[at_row(k * half, i), :] = grad.astype(BF16)
            added = added + grad
        sum_ref[chunk(i), :] = added
        loss_ref[chunk(i), :] = losses
        return carry

    lax.fori_loop(0, half // ROWS, leave, 0)
    middle = out_ref.shape[0] // 2
    send_ref[...] = dot_t(low_ref[...], out_ref[middle : 2 * middle, :]).astype(BF16)


def keep_kernel(low_ref, out_ref, loss_mine, loss_pair, keep_ref, loss_ref, full_ref):
    half = loss_mine.shape[0]
    core = lax.axis_index("tp") % 2
    full_ref[pl.ds(pl.multiple_of(core * half, half), half), :] = loss_mine[...]
    full_ref[pl.ds(pl.multiple_of((1 - core) * half, half), half), :] = loss_pair[...]
    loss_ref[...] = full_ref[...].T[: loss_ref.shape[0], :]
    keep_ref[...] = dot_t(low_ref[...], out_ref[0 : out_ref.shape[0] // 2, :])


def attention_back_kernel(
    head_dim, keep_ref, recv_ref, proj_mine, proj_pair, soft_mine, soft_pair, qkv_mine, qkv_pair,
    stream_ref, gain_ref, sum_ref, part_ref, *refs,
):
    blocks_ref, grad_ref, product_ref, prob_ref, back_mine, back_pair, normin_ref = refs[-7:]
    sends = refs[:-7]
    radix = len(sends) + 1
    digit = lax.axis_index("seq") % radix
    steps, half, _ = stream_ref.shape
    lanes = keep_ref.shape[1] // 2
    chunks = half // ROWS
    pairs = pairs_of(steps)
    scale = head_dim ** (-0.5)
    ones = head_ones(lanes, head_dim)
    for j, (proj, soft, back) in enumerate(
        ((proj_mine, soft_mine, back_mine), (proj_pair, soft_pair, back_pair))
    ):
        span = slice(j * lanes, (j + 1) * lanes)

        def multiply(i, carry):
            rows = [at_row(k * half, i) for k in range(steps)]
            values = [proj[row, 2 * lanes : 3 * lanes] for row in rows]
            for a in range(steps):
                grad = (keep_ref[rows[a], span] + recv_ref[rows[a], span].astype(F32)).astype(BF16)
                grad_ref[rows[a], :] = grad
                for b in range(a + 1):
                    product_ref[at_row(pairs.index((a, b)) * half, i), :] = grad * values[b]
            return carry

        lax.fori_loop(0, chunks, multiply, 0)
        prob_ref[...] = dot(product_ref[...], ones)

        def spread(i, carry):
            rows = [at_row(k * half, i) for k in range(steps)]
            query_grad = [0.0] * steps
            key_grad = [0.0] * steps
            value_grad = [0.0] * steps
            for a in range(steps):
                first = pairs.index((a, 0))
                weights = [soft[at_row((first + b) * half, i), :] for b in range(a + 1)]
                probs = [prob_ref[at_row((first + b) * half, i), :] for b in range(a + 1)]
                inner = functools.reduce(jnp.add, [w * p for w, p in zip(weights, probs)])
                grad = grad_ref[rows[a], :].astype(F32)
                query = proj[rows[a], 0:lanes].astype(F32)
                for b in range(a + 1):
                    score = (weights[b] * (probs[b] - inner) * scale).astype(BF16).astype(F32)
                    key = proj[rows[b], lanes : 2 * lanes].astype(F32)
                    query_grad[a] = query_grad[a] + score * key
                    key_grad[b] = key_grad[b] + score * query
                    value_grad[b] = value_grad[b] + weights[b].astype(BF16).astype(F32) * grad
            for k in range(steps):
                back[rows[k], 0:lanes] = query_grad[k].astype(BF16)
                back[rows[k], lanes : 2 * lanes] = key_grad[k].astype(BF16)
                back[rows[k], 2 * lanes : 3 * lanes] = value_grad[k].astype(BF16)
            return carry

        lax.fori_loop(0, chunks, spread, 0)
    total = 0.0
    for back, weight in ((back_mine, qkv_mine), (back_pair, qkv_pair)):
        for part in range(3):
            total = total + dot_t(back[:, part * lanes : (part + 1) * lanes], weight[part])
    normin_ref[...] = total

    def leave(i, carry):
        part = sum_ref[chunk(i), :]
        for k in range(steps):
            part = part + norm_back(stream_ref[k, chunk(i), :], gain_ref[...], normin_ref[at_row(k * half, i), :])
        part = part.astype(BF16)
        part_ref[chunk(i), :] = part
        count, _, size = blocks_ref.shape
        for j in range(count):
            blocks_ref[j, chunk(i), :] = part[:, j * size : (j + 1) * size]
        return carry

    lax.fori_loop(0, chunks, leave, 0)
    for shift, out in enumerate(sends):
        for w in range(out.shape[0]):
            out[w] = blocks_ref[w * radix + (digit + shift + 1) % radix]


def sum_kernel(first, radix, *refs):
    part_ref, side_ref = refs[:2]
    near, far = refs[2 : first + 1], refs[first + 1 : 2 * first]
    grad_ref, *outs = refs[2 * first : 2 * first + 1 + radix]
    blocks_ref, held_ref = refs[2 * first + 1 + radix :]
    count, _, size = blocks_ref.shape
    rest = count // first
    digit = lax.axis_index("seq") % first
    upper = lax.axis_index("seq") // first % radix
    grad = (part_ref[...].astype(F32) + side_ref[...].astype(F32)).astype(BF16)
    grad_ref[...] = grad
    for j in range(count):
        blocks_ref[j] = grad[:, j * size : (j + 1) * size]
    for w in range(rest):
        held_ref[0, w] = blocks_ref[w * first + digit]
    for place, (one, two) in enumerate(zip(near, far)):
        held_ref[place + 1] = (one[...].astype(F32) + two[...].astype(F32)).astype(BF16)
    for shift, out in enumerate(outs):
        for i in range(first):
            for w in range(rest // radix):
                out[i, w] = held_ref[i, w * radix + (upper + shift) % radix]


def pick_kernel(count, radix, low, *refs):
    digit = lax.axis_index("seq") // low % radix
    for shift, out in enumerate(refs[count:]):
        place = 0
        for item in refs[:count]:
            for q in range(item.shape[0]):
                for w in range(item.shape[1] // radix):
                    out[place, w] = item[q, w * radix + (digit + shift) % radix]
                place += 1


def hidden_grad_kernel(mine_ref, pair_ref, weight_ref, out_ref, full_ref):
    half = mine_ref.shape[0]
    core = lax.axis_index("tp") % 2
    full_ref[pl.ds(pl.multiple_of(core * half, half), half), :] = mine_ref[...]
    full_ref[pl.ds(pl.multiple_of((1 - core) * half, half), half), :] = pair_ref[...]
    out_ref[...] = dot_t(full_ref[...], weight_ref[...]).astype(BF16)


def project_kernel(radices, *refs):
    count = radices[-1]
    out_ref, grads_ref = refs[-2:]
    mine, pair = refs[-2 - 2 * count : -2 - count], refs[-2 - count : -2]
    states = refs[: -2 - 2 * count]
    half = mine[0].shape[2]
    core = lax.axis_index("tp") % 2
    index = lax.axis_index("seq")
    held = mine[0].shape[0]
    for p, (low, high) in enumerate(zip(mine, pair)):
        for q in range(held):
            grads_ref[p * held + q, pl.ds(pl.multiple_of(core * half, half), half), :] = low[q, 0]
            grads_ref[p * held + q, pl.ds(pl.multiple_of((1 - core) * half, half), half), :] = high[q, 0]
    total = 0.0
    for p in range(count * held):
        if len(states) > 1:
            rows = states[p][0]
        else:
            source, left, low = 0, p, 1
            for radix in radices:
                source = source + (index // low + radix - left % radix) % radix * low
                left //= radix
                low *= radix
            rows = states[0][source]
        total = total + lax.dot_general(
            grads_ref[p], rows, (((0,), (0,)), ((), ())), preferred_element_type=F32
        )
    out_ref[...] = total.T


def seq_radices(size):
    radices = []
    while size % 4 == 0:
        radices.append(4)
        size //= 4
    return [size] + radices if size > 1 else radices


def compute(hidden, w_proj, codes, embed_table, w_qkv, w_out, head_table, gain_attn, gain_head):
    frames, steps = codes.shape
    half = frames // 2
    width = w_proj.shape[1]
    head_dim = width // HEADS
    vocab_local = head_table.shape[2]
    lanes = w_qkv.shape[2]
    tp = lax.axis_size("tp")
    seq = lax.axis_size("seq")
    total = float(frames * seq * steps)
    pairs = len(pairs_of(steps))
    rows = steps * half
    gain_attn = gain_attn.reshape(1, width)
    gain_head = gain_head.reshape(1, width)

    def to_peer(value, flip):
        return lax.ppermute(value, "tp", [(i, i ^ flip) for i in range(tp)])

    def along(value, low, radix, shift, flip=0):
        route = []
        for i in range(seq):
            digit = i // low % radix
            there = i + ((digit + shift) % radix - digit) * low
            route += [(i * tp + j, there * tp + (j ^ flip)) for j in range(tp)]
        return lax.ppermute(value, ("seq", "tp"), route)

    cut = lanes // 2
    (out_part,) = call(
        cut_kernel, [((cut, width), BF16)], [pltpu.SemaphoreType.DMA], (w_out,), 6 * 10**9, {0: pltpu.HBM}, limit=4
    )
    out_part = to_peer(out_part, 2)
    partial, partial_other = call(
        context_kernel, [((half, width), F32), ((half, width), BF16)], [],
        (hidden, w_proj), 6 * 10**9, limit=8,
    )
    looked, looked_other = call(
        lookup_kernel, [((steps - 1, half, lanes), BF16)] * 2,
        [pltpu.VMEM((frames, steps), jnp.int32)],
        (codes.T, embed_table), 6 * 10**9, limit=8,
    )
    (partial,) = call(
        join_kernel, [((half, width), BF16)], [],
        (partial, to_peer(partial_other, 1)), partial.size, limit=4,
    )
    partial_side = to_peer(partial, 2)
    looked = [looked, to_peer(looked_other, 1), to_peer(looked, 2), to_peer(looked_other, 3)]

    qkv_mine = w_qkv.transpose(1, 0, 2)
    qkv_pair = to_peer(qkv_mine, 1)
    head_pair = to_peer(head_table, 1)
    out_rest = along(out_part, 1, 2, 1)
    out_parts = (
        w_out, to_peer(w_out, 1), out_part, out_rest,
        to_peer(out_part, 1), to_peer(out_rest, 1),
    )
    radices = seq_radices(seq)
    if seq > 16:
        states = [lax.all_gather(hidden, "seq")]
    else:
        states, low = [hidden[None]], seq
        for radix in reversed(radices):
            low //= radix
            states = [
                item if shift == 0 else along(item, low, radix, shift)
                for item in states
                for shift in range(radix)
            ]

    stream_in, att_mine, proj_mine, proj_pair, soft_mine, soft_pair = call(
        functools.partial(attention_kernel, head_dim),
        [((steps, half, width), F32), ((rows, 2 * lanes), BF16)]
        + [((rows, 3 * lanes), BF16)] * 2 + [((pairs * half, lanes), F32)] * 2,
        [
            pltpu.VMEM((steps - 1, half, width), BF16),
            pltpu.VMEM((rows, width), BF16),
            pltpu.VMEM((pairs * half, lanes), BF16),
            pltpu.VMEM((pairs * half, lanes), F32),
        ],
        (partial, partial_side, *looked, qkv_mine, qkv_pair, gain_attn), 4 * rows * qkv_mine.size,
    )
    att_theirs = to_peer(att_mine, 2)
    out_full, mixed = call(
        mix_kernel, [((tp * lanes, width), BF16), ((steps, half, width), F32)],
        [pltpu.VMEM((rows, width), F32)],
        (att_mine, *out_parts, stream_in), rows * width * width,
    )
    stream_mid, expo, stats = call(
        head_kernel,
        [((steps, half, width), F32), ((steps, 2 * half, 2 * vocab_local), BF16), ((half, 128), F32)],
        [
            pltpu.VMEM((rows, width), F32),
            pltpu.VMEM((rows, width), BF16),
            pltpu.VMEM((steps, half, 2 * vocab_local), F32),
            pltpu.VMEM((frames, steps), jnp.int32),
        ],
        (att_theirs, out_full, mixed, gain_head, codes.T, head_table, head_pair),
        4 * half * head_table.size + rows * width * width,
    )
    stats_side = to_peer(stats, 2)
    (both,) = call(
        head_back_kernel, [((steps, 2 * half, width), F32)], [],
        (expo, head_table, head_pair), 8 * half * head_table.size,
    )
    att_send, mid_low, mid_sum, losses = call(
        functools.partial(mid_kernel, total),
        [((rows, 2 * lanes), BF16), ((rows, width), BF16), ((half, width), F32), ((half, 128), F32)],
        [], (both, stream_mid, gain_head, stats, stats_side, out_full), rows * width * width,
    )
    att_recv = to_peer(att_send, 2)
    att_keep, row_loss = call(
        keep_kernel, [((rows, 2 * lanes), F32), ((steps, frames), F32)], [pltpu.VMEM((frames, 128), F32)],
        (mid_low, out_full, losses, to_peer(losses, 1)), rows * width * width,
    )
    size = width // seq
    first, rest = radices[0], seq // radices[0]
    part, *sends = call(
        functools.partial(attention_back_kernel, head_dim),
        [((half, width), BF16)] + [((rest, half, size), BF16)] * (first - 1),
        [
            pltpu.VMEM((seq, half, size), BF16),
            pltpu.VMEM((rows, lanes), BF16),
            pltpu.VMEM((pairs * half, lanes), BF16),
            pltpu.VMEM((pairs * half, lanes), F32),
            pltpu.VMEM((rows, 3 * lanes), BF16),
            pltpu.VMEM((rows, 3 * lanes), BF16),
            pltpu.VMEM((rows, width), F32),
        ],
        (att_keep, att_recv, proj_mine, proj_pair, soft_mine, soft_pair, qkv_mine, qkv_pair,
         stream_in, gain_attn, mid_sum),
        4 * rows * qkv_mine.size,
    )
    part_side = to_peer(part, 2)
    near = [along(item, 1, first, shift + 1) for shift, item in enumerate(sends)]
    far = [along(item, 1, first, shift + 1, 2) for shift, item in enumerate(sends)]
    part_side, *states = lax.optimization_barrier((part_side, *states))
    context_grad, *sends = call(
        functools.partial(sum_kernel, first, radices[1]),
        [((half, width), BF16)] + [((first, rest // radices[1], half, size), BF16)] * radices[1],
        [pltpu.VMEM((seq, half, size), BF16), pltpu.VMEM((first, rest, half, size), BF16)],
        (part, part_side, *near, *far), part.size, limit=4,
    )
    low = first
    for stage, radix in enumerate(radices):
        if stage == 0:
            continue
        rest //= radix
        if stage > 1:
            held = sum(item.shape[0] for item in owned)
            sends = call(
                functools.partial(pick_kernel, len(owned), radix, low),
                [((held, rest, half, size), BF16)] * radix, [], owned, part.size, limit=4,
            )
        owned = [sends[0]] + [along(item, low, radix, shift + 1) for shift, item in enumerate(sends[1:])]
        low *= radix
    (grad_hidden,) = call(
        hidden_grad_kernel, [((frames, w_proj.shape[0]), BF16)],
        [pltpu.VMEM((frames, width), BF16)],
        (context_grad, to_peer(context_grad, 1), w_proj), 2 * frames * w_proj.size,
    )
    paired = [to_peer(item, 1) for item in owned]
    (grad_proj,) = call(
        functools.partial(project_kernel, tuple(radices)),
        [((hidden.shape[1], size), F32)],
        [pltpu.VMEM((seq, frames, size), BF16)],
        (*states, *owned, *paired), 2 * frames * seq * hidden.shape[1] * size, limit=40 if seq > 16 else 12,
    )
    return (row_loss.T, grad_hidden, grad_proj)


def solution(mesh):
    return jax.shard_map(
        compute,
        mesh=mesh,
        in_specs=(
            P("seq", "tp"),
            P("tp", None),
            P("seq", None),
            P(None, None, "tp"),
            P(None, None, "tp"),
            P("tp", None),
            P(None, None, "tp"),
            P(),
            P(),
        ),
        out_specs=(P("seq", None), P("seq", "tp"), P("tp", "seq")),
        check_vma=False,
    )
```
